256 devices in a mesh: island: 16 (over y_hi, z), inner: 16 (over y_lo, x, core).
Axes of the slice: x: 4, y: 4 (y_hi: 2, y_lo: 2; y = y_hi * 2 + y_lo), z: 8, core: 2. Of those that a mesh axis runs over, the one named last changes fastest.
Arguments:
- island_delta: float32 [16, 2, 8192, 512], P('island', None, 'inner'), may hold values from -200 to 200, as said below
- params: float32 [2, 8192, 512], P(None, 'inner'), may hold values from -6 to 6
- momentum: float32 [2, 8192, 512], P(None, 'inner'), may hold values from -6 to 6
Outputs:
- new_params: float32 [2, 8192, 512], P(None, 'inner')
- new_momentum: float32 [2, 8192, 512], P(None, 'inner')
The draws below stay inside these ranges and needn't reach their ends.
Inputs may be any that keep to these rules, and one draw needn't show every extreme that they name: `island_delta`: entries are finite and of mixed sign.
All inputs are finite; a program needn't handle non-finite values.
Results may differ from the reference program's by a relative error of at most 0.0003.
Values sent between devices are 32-bit elements; how exact they have to be, the bound alone decides.
A program may use at most 64 MiB of HBM per device.

```python
import jax
import jax.numpy as jnp
from jax import lax

D = 8192
HEAD = 128
KVH = 4
ISLANDS = 16


def draw_island_delta(key, part):
    width = KVH * HEAD
    keys = jax.random.split(key, 6)
    rows = jnp.exp(jax.random.uniform(keys[0], (1, 2, D, 1), jnp.float32) * jnp.log(10.0))
    trend = jnp.exp(jnp.arange(D, dtype=jnp.float32) / D * jnp.log(3.0)).reshape(1, 1, D, 1)
    cols = jnp.exp(jax.random.uniform(keys[1], (1, 2, 1, width), jnp.float32) * jnp.log(10.0))
    lift = jnp.exp(jax.random.uniform(keys[2], (ISLANDS, 1, 1, 1), jnp.float32) * jnp.log(3.0))
    scale = rows * trend * cols * lift * 0.1
    values = jax.random.normal(keys[5], (ISLANDS, 2, D, width), jnp.float32) * scale
    return jnp.clip(values, -200.0, 200.0)


def steps_of(key, dims, shards, smallest, top_value):
    gain, own = 1.0, jax.random.fold_in(key, 6)
    for dim, parts in shards:
        draws = jnp.exp(jax.random.uniform(jax.random.fold_in(own, dim), (parts,), jnp.float32, smallest / len(shards), top_value / len(shards)))
        gain = gain * jnp.repeat(draws, dims[dim] // parts).reshape([-1 if axis == dim else 1 for axis in range(len(dims))])
    return gain


def scatter_about(rng, extent, scale, reach, cuts=(), kind=jnp.bfloat16):
    values = jax.random.normal(rng, extent, jnp.float32) * scale
    if len(cuts) > 0:
        values = steps_of(rng, extent, cuts, -0.22, 0.18) * values
    return jnp.clip(values, min=-reach, max=reach).astype(kind)


def setup_inputs(seed: int = 0) -> dict:
    key_of = jax.random.split(jax.random.key(seed), 4)
    island_delta = draw_island_delta(jax.random.fold_in(key_of[3], 71), 0)
    params = scatter_about(key_of[1], (2, D, KVH * HEAD), 1.0, 6.0, ((1, 16),), jnp.float32)
    momentum = scatter_about(key_of[2], (2, D, KVH * HEAD), 1.0, 6.0, ((1, 16),), jnp.float32)
    return dict(island_delta=island_delta, params=params, momentum=momentum)


def reference(island_delta, params, momentum):
    average = lax.optimization_barrier(jnp.sum(island_delta, axis=0)) / ISLANDS
    mean_square = jnp.sum(average * average) / (2 * D * KVH * HEAD)
    factor = jnp.minimum(jnp.float32(1.0), 0.5 / jnp.sqrt(mean_square + 1e-06))
    clipped = factor * average
    new_momentum = 0.9 * momentum + clipped
    new_params = params - 0.7 * (clipped + 0.9 * new_momentum)
    return (new_params, new_momentum)
```

```python
import jax
import jax.numpy as jnp
from jax import lax
from jax.sharding import PartitionSpec as P

D = 8192
HEAD = 128
KVH = 4


def outer_update(average, params, momentum, mean_square):
    factor = jnp.minimum(jnp.float32(1.0), 0.5 / jnp.sqrt(mean_square + 1e-06))
    clipped = factor * average
    new_momentum = 0.9 * momentum + clipped
    new_params = params - 0.7 * (clipped + 0.9 * new_momentum)
    return (new_params, new_momentum)


def body(island_delta, params, momentum):
    replicas = lax.axis_size("island")
    count = 2 * D * KVH * HEAD
    own_delta = island_delta[0]
    part = lax.psum_scatter(own_delta, "island", scatter_dimension=1, tiled=True) / replicas
    part_sq = jnp.sum(part * part)
    average = lax.all_gather(part, "island", axis=1, tiled=True)
    total_sq = lax.psum(part_sq, ("island", "inner"))
    return outer_update(average, params, momentum, total_sq / count)


def solution(mesh):
    in_specs = (P("island", None, "inner", None), P(None, "inner", None), P(None, "inner", None))
    out_specs = (P(None, "inner", None), P(None, "inner", None))
    return jax.shard_map(body, mesh=mesh, in_specs=in_specs, out_specs=out_specs, check_vma=False)
```

```python
import jax
import jax.numpy as jnp
from jax import lax
from jax.sharding import PartitionSpec as P

D = 8192
HEAD = 128
KVH = 4
RING = 8


def outer_update(average, params, momentum, mean_square):
    factor = jnp.minimum(jnp.float32(1.0), 0.5 / jnp.sqrt(mean_square + 1e-06))
    clipped = factor * average
    new_momentum = 0.9 * momentum + clipped
    new_params = params - 0.7 * (clipped + 0.9 * new_momentum)
    return (new_params, new_momentum)


def ring_pairs(islands, shift):
    groups = islands // RING
    return [(g * RING + z, g * RING + (z + shift) % RING) for g in range(groups) for z in range(RING)]


def body(island_delta, params, momentum):
    islands = lax.axis_size("island")
    count = 2 * D * KVH * HEAD
    me = lax.axis_index("island")
    z = me % RING
    own = island_delta[0]
    halves, rows, cols = own.shape
    chunk = rows // RING
    x = own.reshape(halves, RING, chunk, cols)
    right, left = ring_pairs(islands, 1), ring_pairs(islands, RING - 1)

    def take(h, c):
        return lax.dynamic_index_in_dim(x[h], c % RING, axis=0, keepdims=False)

    acc_r = take(0, z - 1)
    acc_l = take(1, z + 1)
    for s in range(RING - 1):
        got_r = lax.ppermute(acc_r, "island", right)
        got_l = lax.ppermute(acc_l, "island", left)
        acc_r = got_r + take(0, z - 2 - s)
        acc_l = got_l + take(1, z + 2 + s)
    mine = jnp.stack([acc_r, acc_l])
    partner = [(i, (i + RING) % islands) for i in range(islands)]
    mine = (mine + lax.ppermute(mine, "island", partner)) / islands
    part_sq = jnp.sum(mine * mine)

    out = jnp.zeros((halves, RING, chunk, cols), jnp.float32)
    out = lax.dynamic_update_index_in_dim(out, mine[:, None], z, axis=1)
    sq = part_sq
    cur_r, cur_l, cur_q = mine[0], mine[1], part_sq
    for s in range(RING - 1):
        cur_r, cur_q = lax.ppermute((cur_r, cur_q), "island", right)
        cur_l = lax.ppermute(cur_l, "island", left)
        sq = sq + cur_q
        out = lax.dynamic_update_slice(out, cur_r[None, None], (0, (z - 1 - s) % RING, 0, 0))
        out = lax.dynamic_update_slice(out, cur_l[None, None], (1, (z + 1 + s) % RING, 0, 0))
    average = out.reshape(halves, rows, cols)
    total_sq = lax.psum(sq, "inner")
    return outer_update(average, params, momentum, total_sq / count)


def solution(mesh):
    in_specs = (P("island", None, "inner", None), P(None, "inner", None), P(None, "inner", None))
    out_specs = (P(None, "inner", None), P(None, "inner", None))
    return jax.shard_map(body, mesh=mesh, in_specs=in_specs, out_specs=out_specs, check_vma=False)
```

```python
import jax
import jax.numpy as jnp
from jax import lax
from jax.sharding import PartitionSpec as P

D = 8192
HEAD = 128
KVH = 4
RING = 8


def outer_update(average, params, momentum, mean_square):
    factor = jnp.minimum(jnp.float32(1.0), 0.5 / jnp.sqrt(mean_square + 1e-06))
    clipped = factor * average
    new_momentum = 0.9 * momentum + clipped
    new_params = params - 0.7 * (clipped + 0.9 * new_momentum)
    return (new_params, new_momentum)


def ring_pairs(islands, shift):
    groups = islands // RING
    return [(g * RING + z, g * RING + (z + shift) % RING) for g in range(groups) for z in range(RING)]


def body(island_delta, params, momentum):
    islands = lax.axis_size("island")
    count = 2 * D * KVH * HEAD
    me = lax.axis_index("island")
    z = me % RING
    own = island_delta[0]
    halves, rows, cols = own.shape
    chunk = rows // RING
    x = own.reshape(halves, RING, chunk, cols)
    right, left = ring_pairs(islands, 1), ring_pairs(islands, RING - 1)

    def take(h, c):
        return lax.dynamic_index_in_dim(x[h], c % RING, axis=0, keepdims=False)

    acc_r = take(0, z - 1)
    acc_l = take(1, z + 1)
    for s in range(RING - 1):
        got_r = lax.ppermute(acc_r, "island", right)
        got_l = lax.ppermute(acc_l, "island", left)
        acc_r = got_r + take(0, z - 2 - s)
        acc_l = got_l + take(1, z + 2 + s)
    mine = jnp.stack([acc_r, acc_l])
    partner = [(i, (i + RING) % islands) for i in range(islands)]
    mine = (mine + lax.ppermute(mine, "island", partner)) / islands
    sq = jnp.sum(mine * mine)
    inner = lax.axis_size("inner")
    flips = [("inner", [(i, i ^ bit) for i in range(inner)]) for bit in (1, 2, 4, 8)]
    flips += [("island", [(g * RING + q, g * RING + (q ^ bit)) for g in range(islands // RING) for q in range(RING)])
              for bit in (1, 2, 4)]

    out = jnp.zeros((halves, RING, chunk, cols), jnp.float32)
    out = lax.dynamic_update_index_in_dim(out, mine[:, None], z, axis=1)
    cur_r, cur_l = mine[0], mine[1]
    for s in range(RING - 1):
        cur_r = lax.ppermute(cur_r, "island", right)
        cur_l = lax.ppermute(cur_l, "island", left)
        axis, pairs = flips[s]
        sq = sq + lax.ppermute(sq, axis, pairs)
        cur_r, cur_l, sq = lax.optimization_barrier((cur_r, cur_l, sq))
        out = lax.dynamic_update_slice(out, cur_r[None, None], (0, (z - 1 - s) % RING, 0, 0))
        out = lax.dynamic_update_slice(out, cur_l[None, None], (1, (z + 1 + s) % RING, 0, 0))
    total_sq = sq
    average = out.reshape(halves, rows, cols)
    return outer_update(average, params, momentum, total_sq / count)


def solution(mesh):
    in_specs = (P("island", None, "inner", None), P(None, "inner", None), P(None, "inner", None))
    out_specs = (P(None, "inner", None), P(None, "inner", None))
    return jax.shard_map(body, mesh=mesh, in_specs=in_specs, out_specs=out_specs, check_vma=False)
```

```python
import jax
import jax.numpy as jnp
from jax import lax
from jax.sharding import PartitionSpec as P

D = 8192
HEAD = 128
KVH = 4
RING = 8


def outer_update(average, params, momentum, mean_square):
    factor = jnp.minimum(jnp.float32(1.0), 0.5 / jnp.sqrt(mean_square + 1e-06))
    clipped = factor * average
    new_momentum = 0.9 * momentum + clipped
    new_params = params - 0.7 * (clipped + 0.9 * new_momentum)
    return (new_params, new_momentum)


def ring_pairs(islands, shift):
    groups = islands // RING
    return [(g * RING + z, g * RING + (z + shift) % RING) for g in range(groups) for z in range(RING)]


def step(island_delta, params, momentum):
    islands = lax.axis_size("island")
    count = 2 * D * KVH * HEAD
    me = lax.axis_index("island")
    z = me % RING
    own = island_delta[0]
    halves, rows, cols = own.shape
    chunk = rows // RING
    x = own.reshape(halves, RING, chunk, cols)
    right, left = ring_pairs(islands, 1), ring_pairs(islands, RING - 1)

    def take(h, c):
        return lax.dynamic_index_in_dim(x[h], c % RING, axis=0, keepdims=False)

    acc_r = take(0, z - 1)
    acc_l = take(1, z + 1)
    for s in range(RING - 1):
        got_r = lax.ppermute(acc_r, "island", right)
        got_l = lax.ppermute(acc_l, "island", left)
        acc_r = got_r + take(0, z - 2 - s)
        acc_l = got_l + take(1, z + 2 + s)
    mine = jnp.stack([acc_r, acc_l])
    partner = [(i, (i + RING) % islands) for i in range(islands)]
    mine = (mine + lax.ppermute(mine, "island", partner)) / islands
    part_sq = jnp.sum(mine * mine)
    part_sq = jnp.where(me < RING, part_sq, jnp.float32(0.0))
    total_sq = lax.psum(jnp.full((128, 128), part_sq), ("island", "inner"))[0, 0]

    out = jnp.zeros((halves, RING, chunk, cols), jnp.float32)
    out = lax.dynamic_update_index_in_dim(out, mine[:, None], z, axis=1)
    cur_r, cur_l = mine[0], mine[1]
    for s in range(RING - 1):
        cur_r = lax.ppermute(cur_r, "island", right)
        cur_l = lax.ppermute(cur_l, "island", left)
        out = lax.dynamic_update_slice(out, cur_r[None, None], (0, (z - 1 - s) % RING, 0, 0))
        out = lax.dynamic_update_slice(out, cur_l[None, None], (1, (z + 1 + s) % RING, 0, 0))
    average = out.reshape(halves, rows, cols)
    return outer_update(average, params, momentum, total_sq / count)


def solution(mesh):
    in_specs = (P("island", None, "inner", None), P(None, "inner", None), P(None, "inner", None))
    out_specs = (P(None, "inner", None), P(None, "inner", None))
    return jax.shard_map(step, mesh=mesh, in_specs=in_specs, out_specs=out_specs, check_vma=False)
```

```python
import jax
import jax.numpy as jnp
from jax import lax
from jax.sharding import PartitionSpec as P

D = 8192
HEAD = 128
KVH = 4
RING = 8


def outer_update(average, params, momentum, mean_square):
    factor = jnp.minimum(jnp.float32(1.0), 0.5 / jnp.sqrt(mean_square + 1e-06))
    clipped = factor * average
    new_momentum = 0.9 * momentum + clipped
    new_params = params - 0.7 * (clipped + 0.9 * new_momentum)
    return (new_params, new_momentum)


def ring_pairs(islands, shift):
    groups = islands // RING
    return [(g * RING + z, g * RING + (z + shift) % RING) for g in range(groups) for z in range(RING)]


def body(island_delta, params, momentum):
    islands = lax.axis_size("island")
    inner = lax.axis_size("inner")
    count = 2 * D * KVH * HEAD
    me = lax.axis_index("island")
    z = me % RING
    own = island_delta[0]
    halves, rows, cols = own.shape
    chunk = rows // RING
    x = own.reshape(halves, RING, chunk, cols)
    right, left = ring_pairs(islands, 1), ring_pairs(islands, RING - 1)
    reach_r, reach_l = (RING - 1) // 2, RING // 2

    def take(c):
        return lax.dynamic_index_in_dim(x, c % RING, axis=1, keepdims=False)

    acc_r = take(z + reach_r)
    acc_l = take(z - reach_l)
    for s in range(reach_l):
        if s < reach_r:
            got_r = lax.ppermute(acc_r, "island", right)
            acc_r = got_r if s == reach_r - 1 else got_r + take(z + reach_r - 1 - s)
        got_l = lax.ppermute(acc_l, "island", left)
        acc_l = got_l if s == reach_l - 1 else got_l + take(z - reach_l + 1 + s)
    mine = take(z) + acc_r + acc_l
    partner = [(i, (i + RING) % islands) for i in range(islands)]
    mine = (mine + lax.ppermute(mine, "island", partner)) / islands

    out = jnp.zeros((halves, RING, chunk, cols), jnp.float32)
    out = lax.dynamic_update_slice(out, mine[:, None], (0, z, 0, 0))
    sq = jnp.sum(mine * mine)
    cur_r, cur_l = mine, mine
    for s in range(reach_l):
        if s < reach_r:
            cur_r = lax.ppermute(cur_r, "island", right)
            sq = sq + jnp.sum(cur_r * cur_r)
            out = lax.dynamic_update_slice(out, cur_r[:, None], (0, (z - 1 - s) % RING, 0, 0))
        cur_l = lax.ppermute(cur_l, "island", left)
        sq = sq + jnp.sum(cur_l * cur_l)
        out = lax.dynamic_update_slice(out, cur_l[:, None], (0, (z + 1 + s) % RING, 0, 0))
    average = out.reshape(halves, rows, cols)
    bit = 1
    while bit < inner:
        sq = sq + lax.ppermute(sq, "inner", [(i, i ^ bit) for i in range(inner)])
        bit *= 2
    return outer_update(average, params, momentum, sq / count)


def solution(mesh):
    in_specs = (P("island", None, "inner", None), P(None, "inner", None), P(None, "inner", None))
    out_specs = (P(None, "inner", None), P(None, "inner", None))
    return jax.shard_map(body, mesh=mesh, in_specs=in_specs, out_specs=out_specs, check_vma=False)
```

```python
import jax
import jax.numpy as jnp
from jax import lax
from jax.sharding import PartitionSpec as P

D = 8192
HEAD = 128
KVH = 4
RING = 8


def outer_update(average, params, momentum, mean_square):
    factor = jnp.minimum(jnp.float32(1.0), 0.5 / jnp.sqrt(mean_square + 1e-06))
    clipped = factor * average
    new_momentum = 0.9 * momentum + clipped
    new_params = params - 0.7 * (clipped + 0.9 * new_momentum)
    return (new_params, new_momentum)


def ring_pairs(islands, shift):
    groups = islands // RING
    return [(g * RING + z, g * RING + (z + shift) % RING) for g in range(groups) for z in range(RING)]


def body(island_delta, params, momentum):
    islands = lax.axis_size("island")
    inner = lax.axis_size("inner")
    count = 2 * D * KVH * HEAD
    me = lax.axis_index("island")
    z = me % RING
    own = island_delta[0]
    halves, rows, cols = own.shape
    chunk = rows // RING
    x = own.reshape(halves, RING, chunk, cols)
    right, left = ring_pairs(islands, 1), ring_pairs(islands, RING - 1)
    reach_r, reach_l = (RING - 1) // 2, RING // 2

    def take(c):
        return lax.dynamic_index_in_dim(x, c % RING, axis=1, keepdims=False)

    acc_r = take(z + reach_r)
    acc_l = take(z - reach_l)
    for s in range(reach_l):
        if s < reach_r:
            got_r = lax.ppermute(acc_r, "island", right)
            acc_r = got_r if s == reach_r - 1 else got_r + take(z + reach_r - 1 - s)
        got_l = lax.ppermute(acc_l, "island", left)
        acc_l = got_l if s == reach_l - 1 else got_l + take(z - reach_l + 1 + s)
    mine = take(z) + acc_r + acc_l
    partner = [(i, (i + RING) % islands) for i in range(islands)]
    mine = (mine + lax.ppermute(mine, "island", partner)) / islands

    out = jnp.zeros((halves, RING, chunk, cols), jnp.float32)
    out = lax.dynamic_update_slice(out, mine[:, None], (0, z, 0, 0))
    sq = jnp.sum(mine * mine)
    cur_r, cur_l = mine, mine
    for s in range(reach_l):
        if s < reach_r:
            cur_r = lax.ppermute(cur_r, "island", right)
            sq = sq + jnp.sum(cur_r * cur_r)
            out = lax.dynamic_update_slice(out, cur_r[:, None], (0, (z - 1 - s) % RING, 0, 0))
        cur_l = lax.ppermute(cur_l, "island", left)
        sq = sq + jnp.sum(cur_l * cur_l)
        out = lax.dynamic_update_slice(out, cur_l[:, None], (0, (z + 1 + s) % RING, 0, 0))
    average = out.reshape(halves, rows, cols)
    sq = jnp.sum(lax.all_to_all(jnp.full((inner, 1), sq), "inner", 0, 0, tiled=True))
    return outer_update(average, params, momentum, sq / count)


def solution(mesh):
    in_specs = (P("island", None, "inner", None), P(None, "inner", None), P(None, "inner", None))
    out_specs = (P(None, "inner", None), P(None, "inner", None))
    return jax.shard_map(body, mesh=mesh, in_specs=in_specs, out_specs=out_specs, check_vma=False)
```

```python
import functools

import jax
import jax.numpy as jnp
from jax import lax
from jax.experimental import pallas as pl
from jax.experimental.pallas import tpu as pltpu
from jax.sharding import PartitionSpec as P

D = 8192
HEAD = 128
KVH = 4
RING = 8
MESH = pl.DeviceIdType.MESH
REACH_R, REACH_L = (RING - 1) // 2, RING // 2
RS_R, RS_L = 0, REACH_R
Y = REACH_R + REACH_L
AG_R = Y + 1
AG_L = AG_R + REACH_R
COPIES = AG_L + REACH_L


def outer_update(average, params, momentum, mean_square):
    factor = jnp.minimum(jnp.float32(1.0), 0.5 / jnp.sqrt(mean_square + 1e-06))
    clipped = factor * average
    new_momentum = 0.9 * momentum + clipped
    new_params = params - 0.7 * (clipped + 0.9 * new_momentum)
    return (new_params, new_momentum)


def ring_kernel(islands, x_ref, out_ref, sbuf, rbuf, ssem, rsem):
    chunk = x_ref.shape[1] // RING
    me = lax.axis_index("island")
    col = lax.axis_index("inner")
    z = me % RING
    base = me - z
    right = base + (z + 1) % RING
    left = base + (z + RING - 1) % RING
    partner = (me + RING) % islands

    def rows(k):
        return pl.ds(pl.multiple_of(((z + k) % RING) * chunk, chunk), chunk)

    def send(k, src, dst, target):
        cp = pltpu.make_async_remote_copy(
            src_ref=src, dst_ref=dst, send_sem=ssem.at[k], recv_sem=rsem.at[k],
            device_id={"island": target}, device_id_type=MESH)
        cp.start()
        return cp

    barrier = pltpu.get_barrier_semaphore()
    for target in (left, right, partner):
        pl.semaphore_signal(barrier, inc=1, device_id={"island": target}, device_id_type=MESH)
    pl.semaphore_wait(barrier, 3)

    cr = send(RS_R, x_ref.at[:, rows(REACH_R)], rbuf.at[RS_R], right)
    cl = send(RS_L, x_ref.at[:, rows(RING - REACH_L)], rbuf.at[RS_L], left)
    for s in range(REACH_L):
        if s < REACH_R:
            cr.wait()
            if s < REACH_R - 1:
                k = RS_R + s
                sbuf[k + 1] = rbuf[k] + x_ref[:, rows(REACH_R - 1 - s)]
                cr = send(k + 1, sbuf.at[k + 1], rbuf.at[k + 1], right)
        cl.wait()
        if s < REACH_L - 1:
            k = RS_L + s
            sbuf[k + 1] = rbuf[k] + x_ref[:, rows(RING - REACH_L + 1 + s)]
            cl = send(k + 1, sbuf.at[k + 1], rbuf.at[k + 1], left)

    sbuf[Y] = x_ref[:, rows(0)] + rbuf[RS_R + REACH_R - 1] + rbuf[RS_L + REACH_L - 1]
    cy = send(Y, sbuf.at[Y], rbuf.at[Y], partner)
    cy.wait()
    out_ref[:, rows(0)] = (sbuf[Y] + rbuf[Y]) / islands

    cr = cl = None
    for s in range(REACH_L):
        if s < REACH_R:
            if cr is not None:
                cr.wait()
            cr = send(AG_R + s, out_ref.at[:, rows(RING - s)], out_ref.at[:, rows(RING - s)], right)
        if cl is not None:
            cl.wait()
        cl = send(AG_L + s, out_ref.at[:, rows(s)], out_ref.at[:, rows(s)], left)
    cr.wait()
    cl.wait()


def all_reduce(own, islands):
    halves, rows, cols = own.shape
    chunk = rows // RING
    return pl.pallas_call(
        functools.partial(ring_kernel, islands),
        out_shape=jax.ShapeDtypeStruct(own.shape, own.dtype),
        in_specs=[pl.BlockSpec(memory_space=pltpu.VMEM)],
        out_specs=pl.BlockSpec(memory_space=pltpu.VMEM),
        scratch_shapes=[
            pltpu.VMEM((COPIES, halves, chunk, cols), own.dtype),
            pltpu.VMEM((COPIES, halves, chunk, cols), own.dtype),
            pltpu.SemaphoreType.DMA((COPIES,)),
            pltpu.SemaphoreType.DMA((COPIES,)),
        ],
        compiler_params=pltpu.CompilerParams(
            collective_id=0, has_side_effects=True, vmem_limit_bytes=48 * 1024 * 1024),
    )(own)


def body(island_delta, params, momentum):
    islands = lax.axis_size("island")
    inner = lax.axis_size("inner")
    count = 2 * D * KVH * HEAD
    average = all_reduce(island_delta[0], islands)
    sq = jnp.sum(average * average)
    sq = jnp.sum(lax.all_to_all(jnp.full((inner, 1), sq), "inner", 0, 0, tiled=True))
    return outer_update(average, params, momentum, sq / count)


def solution(mesh):
    in_specs = (P("island", None, "inner", None), P(None, "inner", None), P(None, "inner", None))
    out_specs = (P(None, "inner", None), P(None, "inner", None))
    return jax.shard_map(body, mesh=mesh, in_specs=in_specs, out_specs=out_specs, check_vma=False)
```

```python
import functools

import jax
import jax.numpy as jnp
from jax import lax
from jax.experimental import pallas as pl
from jax.experimental.pallas import tpu as pltpu
from jax.sharding import PartitionSpec as P

D = 8192
HEAD = 128
KVH = 4
RING = 8
MESH = pl.DeviceIdType.MESH
REACH_R, REACH_L = (RING - 1) // 2, RING // 2
RS_R, RS_L = 0, REACH_R
Y = REACH_R + REACH_L
AG_R = Y + 1
AG_L = AG_R + REACH_R
COPIES = AG_L + REACH_L


def outer_update(average, params, momentum, mean_square):
    factor = jnp.minimum(jnp.float32(1.0), 0.5 / jnp.sqrt(mean_square + 1e-06))
    clipped = factor * average
    new_momentum = 0.9 * momentum + clipped
    new_params = params - 0.7 * (clipped + 0.9 * new_momentum)
    return (new_params, new_momentum)


def ring_kernel(islands, inner, x_ref, out_ref, sq_ref, sbuf, rbuf, ssem, rsem, sq_in, sq_ssem, sq_rsem):
    chunk = x_ref.shape[1] // RING
    me = lax.axis_index("island")
    col = lax.axis_index("inner")
    z = me % RING
    base = me - z
    right = base + (z + 1) % RING
    left = base + (z + RING - 1) % RING
    partner = (me + RING) % islands

    def rows(k):
        return pl.ds(pl.multiple_of(((z + k) % RING) * chunk, chunk), chunk)

    def send(k, src, dst, target):
        cp = pltpu.make_async_remote_copy(
            src_ref=src, dst_ref=dst, send_sem=ssem.at[k], recv_sem=rsem.at[k],
            device_id={"island": target}, device_id_type=MESH)
        cp.start()
        return cp

    barrier = pltpu.get_barrier_semaphore()
    for target in (left, right, partner):
        pl.semaphore_signal(barrier, inc=1, device_id={"island": target}, device_id_type=MESH)
    for o in range(1, inner):
        pl.semaphore_signal(barrier, inc=1, device_id={"inner": (col + o) % inner}, device_id_type=MESH)
    pl.semaphore_wait(barrier, 3 + inner - 1)

    cr = send(RS_R, x_ref.at[:, rows(REACH_R)], rbuf.at[RS_R], right)
    cl = send(RS_L, x_ref.at[:, rows(RING - REACH_L)], rbuf.at[RS_L], left)
    for s in range(REACH_L):
        if s < REACH_R:
            cr.wait()
            if s < REACH_R - 1:
                k = RS_R + s
                sbuf[k + 1] = rbuf[k] + x_ref[:, rows(REACH_R - 1 - s)]
                cr = send(k + 1, sbuf.at[k + 1], rbuf.at[k + 1], right)
        cl.wait()
        if s < REACH_L - 1:
            k = RS_L + s
            sbuf[k + 1] = rbuf[k] + x_ref[:, rows(RING - REACH_L + 1 + s)]
            cl = send(k + 1, sbuf.at[k + 1], rbuf.at[k + 1], left)

    sbuf[Y] = x_ref[:, rows(0)] + rbuf[RS_R + REACH_R - 1] + rbuf[RS_L + REACH_L - 1]
    cy = send(Y, sbuf.at[Y], rbuf.at[Y], partner)
    cy.wait()
    out_ref[:, rows(0)] = (sbuf[Y] + rbuf[Y]) / islands

    cr = cl = None
    for s in range(REACH_L):
        if s < REACH_R:
            if cr is not None:
                cr.wait()
            cr = send(AG_R + s, out_ref.at[:, rows(RING - s)], out_ref.at[:, rows(RING - s)], right)
        if cl is not None:
            cl.wait()
        cl = send(AG_L + s, out_ref.at[:, rows(s)], out_ref.at[:, rows(s)], left)
    cr.wait()
    cl.wait()

    block = out_ref[...]
    sq_in[col] = jnp.full(sq_in.shape[1:], jnp.sum(block * block), jnp.float32)
    sends = []
    for o in range(1, inner):
        cp = pltpu.make_async_remote_copy(
            src_ref=sq_in.at[col], dst_ref=sq_in.at[col], send_sem=sq_ssem.at[o], recv_sem=sq_rsem.at[col],
            device_id={"inner": (col + o) % inner}, device_id_type=MESH)
        cp.start()
        sends.append(cp)
    for o in range(1, inner):
        src = (col + inner - o) % inner
        pltpu.make_async_remote_copy(
            src_ref=sq_in.at[src], dst_ref=sq_in.at[src], send_sem=sq_ssem.at[o], recv_sem=sq_rsem.at[src],
            device_id={"inner": src}, device_id_type=MESH).wait_recv()
    for cp in sends:
        cp.wait_send()
    total = sq_in[0]
    for j in range(1, inner):
        total = total + sq_in[j]
    sq_ref[...] = total


def all_reduce(own, islands, inner):
    halves, rows, cols = own.shape
    chunk = rows // RING
    return pl.pallas_call(
        functools.partial(ring_kernel, islands, inner),
        out_shape=(jax.ShapeDtypeStruct(own.shape, own.dtype), jax.ShapeDtypeStruct((8, 128), jnp.float32)),
        in_specs=[pl.BlockSpec(memory_space=pltpu.VMEM)],
        out_specs=(pl.BlockSpec(memory_space=pltpu.VMEM), pl.BlockSpec(memory_space=pltpu.VMEM)),
        scratch_shapes=[
            pltpu.VMEM((COPIES, halves, chunk, cols), own.dtype),
            pltpu.VMEM((COPIES, halves, chunk, cols), own.dtype),
            pltpu.SemaphoreType.DMA((COPIES,)),
            pltpu.SemaphoreType.DMA((COPIES,)),
            pltpu.VMEM((inner, 8, 128), jnp.float32),
            pltpu.SemaphoreType.DMA((inner,)),
            pltpu.SemaphoreType.DMA((inner,)),
        ],
        compiler_params=pltpu.CompilerParams(
            collective_id=0, has_side_effects=True, vmem_limit_bytes=48 * 1024 * 1024),
    )(own)


def body(island_delta, params, momentum):
    islands = lax.axis_size("island")
    inner = lax.axis_size("inner")
    count = 2 * D * KVH * HEAD
    average, sq = all_reduce(island_delta[0], islands, inner)
    return outer_update(average, params, momentum, sq[0, 0] / count)


def solution(mesh):
    in_specs = (P("island", None, "inner", None), P(None, "inner", None), P(None, "inner", None))
    out_specs = (P(None, "inner", None), P(None, "inner", None))
    return jax.shard_map(body, mesh=mesh, in_specs=in_specs, out_specs=out_specs, check_vma=False)
```

```python
import functools

import jax
import jax.numpy as jnp
from jax import lax
from jax.experimental import pallas as pl
from jax.experimental.pallas import tpu as pltpu
from jax.sharding import PartitionSpec as P

D = 8192
HEAD = 128
KVH = 4
RING = 8
MESH = pl.DeviceIdType.MESH
REACH_R, REACH_L = (RING - 1) // 2, RING // 2
RS_R, RS_L = 0, REACH_R
Y = REACH_R + REACH_L
AG_R = Y + 1
AG_L = AG_R + REACH_R
COPIES = AG_L + REACH_L


def outer_update(average, params, momentum, mean_square):
    factor = jnp.minimum(jnp.float32(1.0), 0.5 / jnp.sqrt(mean_square + 1e-06))
    clipped = factor * average
    new_momentum = 0.9 * momentum + clipped
    new_params = params - 0.7 * (clipped + 0.9 * new_momentum)
    return (new_params, new_momentum)


def ring_kernel(islands, inner, x_ref, out_ref, sq_ref, sbuf, rbuf, ssem, rsem, sq_in, sq_ssem, sq_rsem, sq_chunk):
    chunk = x_ref.shape[1] // RING
    me = lax.axis_index("island")
    col = lax.axis_index("inner")
    z = me % RING
    base = me - z
    right = base + (z + 1) % RING
    left = base + (z + RING - 1) % RING
    partner = (me + RING) % islands

    def rows(k):
        return pl.ds(pl.multiple_of(((z + k) % RING) * chunk, chunk), chunk)

    def send(k, src, dst, target):
        cp = pltpu.make_async_remote_copy(
            src_ref=src, dst_ref=dst, send_sem=ssem.at[k], recv_sem=rsem.at[k],
            device_id={"island": target}, device_id_type=MESH)
        cp.start()
        return cp

    barrier = pltpu.get_barrier_semaphore()
    for target in (left, right, partner):
        pl.semaphore_signal(barrier, inc=1, device_id={"island": target}, device_id_type=MESH)
    for o in range(1, inner):
        pl.semaphore_signal(barrier, inc=1, device_id={"inner": (col + o) % inner}, device_id_type=MESH)
    pl.semaphore_wait(barrier, 3 + inner - 1)

    cr = send(RS_R, x_ref.at[:, rows(REACH_R)], rbuf.at[RS_R], right)
    cl = send(RS_L, x_ref.at[:, rows(RING - REACH_L)], rbuf.at[RS_L], left)
    for s in range(REACH_L):
        if s < REACH_R:
            cr.wait()
            if s < REACH_R - 1:
                k = RS_R + s
                sbuf[k + 1] = rbuf[k] + x_ref[:, rows(REACH_R - 1 - s)]
                cr = send(k + 1, sbuf.at[k + 1], rbuf.at[k + 1], right)
        cl.wait()
        if s < REACH_L - 1:
            k = RS_L + s
            sbuf[k + 1] = rbuf[k] + x_ref[:, rows(RING - REACH_L + 1 + s)]
            cl = send(k + 1, sbuf.at[k + 1], rbuf.at[k + 1], left)

    sbuf[Y] = x_ref[:, rows(0)] + rbuf[RS_R + REACH_R - 1] + rbuf[RS_L + REACH_L - 1]
    cy = send(Y, sbuf.at[Y], rbuf.at[Y], partner)
    cy.wait()
    out_ref[:, rows(0)] = (sbuf[Y] + rbuf[Y]) / islands

    def square(k):
        part = out_ref[:, rows(k)]
        sq_chunk[(z + k) % RING] = jnp.full(sq_chunk.shape[1:], jnp.sum(part * part), jnp.float32)

    cr = cl = None
    for s in range(REACH_L):
        if s < REACH_R:
            if cr is not None:
                cr.wait()
            cr = send(AG_R + s, out_ref.at[:, rows(RING - s)], out_ref.at[:, rows(RING - s)], right)
        if cl is not None:
            cl.wait()
        cl = send(AG_L + s, out_ref.at[:, rows(s)], out_ref.at[:, rows(s)], left)
        if s < REACH_R:
            square(RING - s)
        if s > 0:
            square(s)
    cr.wait()
    square(RING - REACH_R)
    cl.wait()
    square(REACH_L)

    mine = sq_chunk[0]
    for c in range(1, RING):
        mine = mine + sq_chunk[c]
    sq_in[col] = mine
    sends = []
    for o in range(1, inner):
        cp = pltpu.make_async_remote_copy(
            src_ref=sq_in.at[col], dst_ref=sq_in.at[col], send_sem=sq_ssem.at[o], recv_sem=sq_rsem.at[col],
            device_id={"inner": (col + o) % inner}, device_id_type=MESH)
        cp.start()
        sends.append(cp)
    for o in range(1, inner):
        src = (col + inner - o) % inner
        pltpu.make_async_remote_copy(
            src_ref=sq_in.at[src], dst_ref=sq_in.at[src], send_sem=sq_ssem.at[o], recv_sem=sq_rsem.at[src],
            device_id={"inner": src}, device_id_type=MESH).wait_recv()
    for cp in sends:
        cp.wait_send()
    total = sq_in[0]
    for j in range(1, inner):
        total = total + sq_in[j]
    sq_ref[...] = total


def all_reduce(own, islands, inner):
    halves, rows, cols = own.shape
    chunk = rows // RING
    return pl.pallas_call(
        functools.partial(ring_kernel, islands, inner),
        out_shape=(jax.ShapeDtypeStruct(own.shape, own.dtype), jax.ShapeDtypeStruct((8, 128), jnp.float32)),
        in_specs=[pl.BlockSpec(memory_space=pltpu.VMEM)],
        out_specs=(pl.BlockSpec(memory_space=pltpu.VMEM), pl.BlockSpec(memory_space=pltpu.VMEM)),
        scratch_shapes=[
            pltpu.VMEM((COPIES, halves, chunk, cols), own.dtype),
            pltpu.VMEM((COPIES, halves, chunk, cols), own.dtype),
            pltpu.SemaphoreType.DMA((COPIES,)),
            pltpu.SemaphoreType.DMA((COPIES,)),
            pltpu.VMEM((inner, 8, 128), jnp.float32),
            pltpu.SemaphoreType.DMA((inner,)),
            pltpu.SemaphoreType.DMA((inner,)),
            pltpu.VMEM((RING, 8, 128), jnp.float32),
        ],
        compiler_params=pltpu.CompilerParams(
            collective_id=0, has_side_effects=True, vmem_limit_bytes=48 * 1024 * 1024),
    )(own)


def body(island_delta, params, momentum):
    islands = lax.axis_size("island")
    inner = lax.axis_size("inner")
    count = 2 * D * KVH * HEAD
    average, sq = all_reduce(island_delta[0], islands, inner)
    return outer_update(average, params, momentum, sq[0, 0] / count)


def solution(mesh):
    in_specs = (P("island", None, "inner", None), P(None, "inner", None), P(None, "inner", None))
    out_specs = (P(None, "inner", None), P(None, "inner", None))
    return jax.shard_map(body, mesh=mesh, in_specs=in_specs, out_specs=out_specs, check_vma=False)
```

```python
import functools

import jax
import jax.numpy as jnp
from jax import lax
from jax.experimental import pallas as pl
from jax.experimental.pallas import tpu as pltpu
from jax.sharding import PartitionSpec as P

D = 8192
HEAD = 128
KVH = 4
RING = 8
MESH = pl.DeviceIdType.MESH
REACH_R, REACH_L = (RING - 1) // 2, RING // 2
RS_R, RS_L = 0, REACH_R
Y = REACH_R + REACH_L
AG_R = Y + 1
AG_L = AG_R + REACH_R
COPIES = AG_L + REACH_L


def outer_update(average, params, momentum, mean_square):
    factor = jnp.minimum(jnp.float32(1.0), 0.5 / jnp.sqrt(mean_square + 1e-06))
    clipped = factor * average
    new_momentum = 0.9 * momentum + clipped
    new_params = params - 0.7 * (clipped + 0.9 * new_momentum)
    return (new_params, new_momentum)


def ring_kernel(islands, inner, x_ref, out_ref, sq_ref, sbuf, rbuf, ssem, rsem, sq_in, sq_ssem, sq_rsem, sq_z, z_ssem, z_rsem):
    chunk = x_ref.shape[1] // RING
    me = lax.axis_index("island")
    col = lax.axis_index("inner")
    z = me % RING
    base = me - z
    right = base + (z + 1) % RING
    left = base + (z + RING - 1) % RING
    partner = (me + RING) % islands

    def rows(k):
        return pl.ds(pl.multiple_of(((z + k) % RING) * chunk, chunk), chunk)

    def send(k, src, dst, target):
        cp = pltpu.make_async_remote_copy(
            src_ref=src, dst_ref=dst, send_sem=ssem.at[k], recv_sem=rsem.at[k],
            device_id={"island": target}, device_id_type=MESH)
        cp.start()
        return cp

    barrier = pltpu.get_barrier_semaphore()
    for target in (left, right, partner):
        pl.semaphore_signal(barrier, inc=1, device_id={"island": target}, device_id_type=MESH)
    for o in range(1, inner):
        pl.semaphore_signal(barrier, inc=1, device_id={"inner": (col + o) % inner}, device_id_type=MESH)
    for o in range(2, RING - 1):
        pl.semaphore_signal(barrier, inc=1, device_id={"island": base + (z + o) % RING}, device_id_type=MESH)
    pl.semaphore_wait(barrier, 3 + inner - 1 + RING - 3)

    cr = send(RS_R, x_ref.at[:, rows(REACH_R)], rbuf.at[RS_R], right)
    cl = send(RS_L, x_ref.at[:, rows(RING - REACH_L)], rbuf.at[RS_L], left)
    for s in range(REACH_L):
        if s < REACH_R:
            cr.wait()
            if s < REACH_R - 1:
                k = RS_R + s
                sbuf[k + 1] = rbuf[k] + x_ref[:, rows(REACH_R - 1 - s)]
                cr = send(k + 1, sbuf.at[k + 1], rbuf.at[k + 1], right)
        cl.wait()
        if s < REACH_L - 1:
            k = RS_L + s
            sbuf[k + 1] = rbuf[k] + x_ref[:, rows(RING - REACH_L + 1 + s)]
            cl = send(k + 1, sbuf.at[k + 1], rbuf.at[k + 1], left)

    sbuf[Y] = x_ref[:, rows(0)] + rbuf[RS_R + REACH_R - 1] + rbuf[RS_L + REACH_L - 1]
    cy = send(Y, sbuf.at[Y], rbuf.at[Y], partner)
    cy.wait()
    mine = (sbuf[Y] + rbuf[Y]) / islands
    out_ref[:, rows(0)] = mine

    sq_in[col] = jnp.full(sq_in.shape[1:], jnp.sum(mine * mine), jnp.float32)
    inner_sends = []
    for o in range(1, inner):
        cp = pltpu.make_async_remote_copy(
            src_ref=sq_in.at[col], dst_ref=sq_in.at[col], send_sem=sq_ssem.at[o], recv_sem=sq_rsem.at[col],
            device_id={"inner": (col + o) % inner}, device_id_type=MESH)
        cp.start()
        inner_sends.append(cp)
    z_sends = []

    def to_z_peers():
        for o in range(1, inner):
            src = (col + inner - o) % inner
            pltpu.make_async_remote_copy(
                src_ref=sq_in.at[src], dst_ref=sq_in.at[src], send_sem=sq_ssem.at[o], recv_sem=sq_rsem.at[src],
                device_id={"inner": src}, device_id_type=MESH).wait_recv()
        for cp in inner_sends:
            cp.wait_send()
        over_inner = sq_in[0]
        for j in range(1, inner):
            over_inner = over_inner + sq_in[j]
        sq_z[z] = over_inner
        for o in range(1, RING):
            cp = pltpu.make_async_remote_copy(
                src_ref=sq_z.at[z], dst_ref=sq_z.at[z], send_sem=z_ssem.at[o], recv_sem=z_rsem.at[z],
                device_id={"island": base + (z + o) % RING}, device_id_type=MESH)
            cp.start()
            z_sends.append(cp)

    cr = cl = None
    for s in range(REACH_L):
        if s == 2:
            to_z_peers()
        if s < REACH_R:
            if cr is not None:
                cr.wait()
            cr = send(AG_R + s, out_ref.at[:, rows(RING - s)], out_ref.at[:, rows(RING - s)], right)
        if cl is not None:
            cl.wait()
        cl = send(AG_L + s, out_ref.at[:, rows(s)], out_ref.at[:, rows(s)], left)
    cr.wait()
    cl.wait()

    for o in range(1, RING):
        src = (z + RING - o) % RING
        pltpu.make_async_remote_copy(
            src_ref=sq_z.at[src], dst_ref=sq_z.at[src], send_sem=z_ssem.at[o], recv_sem=z_rsem.at[src],
            device_id={"island": base + src}, device_id_type=MESH).wait_recv()
    for cp in z_sends:
        cp.wait_send()
    total = sq_z[0]
    for c in range(1, RING):
        total = total + sq_z[c]
    sq_ref[...] = total


def all_reduce(own, islands, inner):
    halves, rows, cols = own.shape
    chunk = rows // RING
    return pl.pallas_call(
        functools.partial(ring_kernel, islands, inner),
        out_shape=(jax.ShapeDtypeStruct(own.shape, own.dtype), jax.ShapeDtypeStruct((8, 128), jnp.float32)),
        in_specs=[pl.BlockSpec(memory_space=pltpu.VMEM)],
        out_specs=(pl.BlockSpec(memory_space=pltpu.VMEM), pl.BlockSpec(memory_space=pltpu.VMEM)),
        scratch_shapes=[
            pltpu.VMEM((COPIES, halves, chunk, cols), own.dtype),
            pltpu.VMEM((COPIES, halves, chunk, cols), own.dtype),
            pltpu.SemaphoreType.DMA((COPIES,)),
            pltpu.SemaphoreType.DMA((COPIES,)),
            pltpu.VMEM((inner, 8, 128), jnp.float32),
            pltpu.SemaphoreType.DMA((inner,)),
            pltpu.SemaphoreType.DMA((inner,)),
            pltpu.VMEM((RING, 8, 128), jnp.float32),
            pltpu.SemaphoreType.DMA((RING,)),
            pltpu.SemaphoreType.DMA((RING,)),
        ],
        compiler_params=pltpu.CompilerParams(
            collective_id=0, has_side_effects=True, vmem_limit_bytes=48 * 1024 * 1024),
    )(own)


def body(island_delta, params, momentum):
    islands = lax.axis_size("island")
    inner = lax.axis_size("inner")
    count = 2 * D * KVH * HEAD
    average, sq = all_reduce(island_delta[0], islands, inner)
    return outer_update(average, params, momentum, sq[0, 0] / count)


def solution(mesh):
    in_specs = (P("island", None, "inner", None), P(None, "inner", None), P(None, "inner", None))
    out_specs = (P(None, "inner", None), P(None, "inner", None))
    return jax.shard_map(body, mesh=mesh, in_specs=in_specs, out_specs=out_specs, check_vma=False)
```

```python
import functools

import jax
import jax.numpy as jnp
from jax import lax
from jax.experimental import pallas as pl
from jax.experimental.pallas import tpu as pltpu
from jax.sharding import PartitionSpec as P

D = 8192
HEAD = 128
KVH = 4
RING = 8
MESH = pl.DeviceIdType.MESH
CHAINS = ((1, 0, RING // 2), (-1, 0, (RING - 1) // 2), (1, 1, (RING - 1) // 2), (-1, 1, RING // 2))
RS_BASE = tuple(sum(c[2] for c in CHAINS[:i]) for i in range(len(CHAINS)))
Y = sum(c[2] for c in CHAINS)
AG_BASE = tuple(Y + 1 + base for base in RS_BASE)
COPIES = 2 * Y + 1


def outer_update(average, params, momentum, mean_square):
    factor = jnp.minimum(jnp.float32(1.0), 0.5 / jnp.sqrt(mean_square + 1e-06))
    clipped = factor * average
    new_momentum = 0.9 * momentum + clipped
    new_params = params - 0.7 * (clipped + 0.9 * new_momentum)
    return (new_params, new_momentum)


def ring_kernel(islands, inner, x_ref, out_ref, sq_ref, sbuf, rbuf, ssem, rsem, sq_in, sq_ssem, sq_rsem, sq_z, z_ssem, z_rsem):
    chunk = x_ref.shape[1] // RING
    me = lax.axis_index("island")
    col = lax.axis_index("inner")
    z = me % RING
    base = me - z
    right = base + (z + 1) % RING
    left = base + (z + RING - 1) % RING
    partner = (me + RING) % islands

    half = chunk // 2

    def rows(k, h=None):
        start = ((z + k + 2 * RING) % RING) * chunk
        if h is None:
            return pl.ds(pl.multiple_of(start, chunk), chunk)
        return pl.ds(pl.multiple_of(start + h * half, half), half)

    def send(k, src, dst, target):
        cp = pltpu.make_async_remote_copy(
            src_ref=src, dst_ref=dst, send_sem=ssem.at[k], recv_sem=rsem.at[k],
            device_id={"island": target}, device_id_type=MESH)
        cp.start()
        return cp

    barrier = pltpu.get_barrier_semaphore()
    for target in (left, right, partner):
        pl.semaphore_signal(barrier, inc=1, device_id={"island": target}, device_id_type=MESH)
    for o in range(1, inner):
        pl.semaphore_signal(barrier, inc=1, device_id={"inner": (col + o) % inner}, device_id_type=MESH)
    for o in range(2, RING - 1):
        pl.semaphore_signal(barrier, inc=1, device_id={"island": base + (z + o) % RING}, device_id_type=MESH)
    pl.semaphore_wait(barrier, 3 + inner - 1 + RING - 3)

    pending = [None] * len(CHAINS)
    for s in range(RING // 2):
        for i, (d, h, r) in enumerate(CHAINS):
            if s >= r:
                continue
            k = RS_BASE[i] + s
            target = right if d > 0 else left
            if s == 0:
                pending[i] = send(k, x_ref.at[:, rows(d * r, h)], rbuf.at[k, :, pl.ds(0, half)], target)
                continue
            pending[i].wait()
            sbuf[k, :, pl.ds(0, half)] = rbuf[k - 1, :, pl.ds(0, half)] + x_ref[:, rows(d * (r - s), h)]
            pending[i] = send(k, sbuf.at[k, :, pl.ds(0, half)], rbuf.at[k, :, pl.ds(0, half)], target)
    for cp in pending:
        cp.wait()
    for h in range(2):
        own = x_ref[:, rows(0, h)]
        for i, (d, hh, r) in enumerate(CHAINS):
            if hh == h:
                own = own + rbuf[RS_BASE[i] + r - 1, :, pl.ds(0, half)]
        sbuf[Y, :, pl.ds(h * half, half)] = own
    cy = send(Y, sbuf.at[Y], rbuf.at[Y], partner)
    cy.wait()
    mine = (sbuf[Y] + rbuf[Y]) / islands
    out_ref[:, rows(0)] = mine

    sq_in[col] = jnp.full(sq_in.shape[1:], jnp.sum(mine * mine), jnp.float32)
    inner_sends = []
    for o in range(1, inner):
        cp = pltpu.make_async_remote_copy(
            src_ref=sq_in.at[col], dst_ref=sq_in.at[col], send_sem=sq_ssem.at[o], recv_sem=sq_rsem.at[col],
            device_id={"inner": (col + o) % inner}, device_id_type=MESH)
        cp.start()
        inner_sends.append(cp)
    z_sends = []

    def to_z_peers():
        for o in range(1, inner):
            src = (col + inner - o) % inner
            pltpu.make_async_remote_copy(
                src_ref=sq_in.at[src], dst_ref=sq_in.at[src], send_sem=sq_ssem.at[o], recv_sem=sq_rsem.at[src],
                device_id={"inner": src}, device_id_type=MESH).wait_recv()
        for cp in inner_sends:
            cp.wait_send()
        over_inner = sq_in[0]
        for j in range(1, inner):
            over_inner = over_inner + sq_in[j]
        sq_z[z] = over_inner
        for o in range(1, RING):
            cp = pltpu.make_async_remote_copy(
                src_ref=sq_z.at[z], dst_ref=sq_z.at[z], send_sem=z_ssem.at[o], recv_sem=z_rsem.at[z],
                device_id={"island": base + (z + o) % RING}, device_id_type=MESH)
            cp.start()
            z_sends.append(cp)

    for s in range(RING // 2):
        if s == 2:
            to_z_peers()
        for i, (d, h, r) in enumerate(CHAINS):
            if s >= r:
                continue
            if s > 0:
                pending[i].wait()
            k = AG_BASE[i] + s
            place = out_ref.at[:, rows(-d * s, h)]
            pending[i] = send(k, place, place, right if d > 0 else left)
    for cp in pending:
        cp.wait()

    for o in range(1, RING):
        src = (z + RING - o) % RING
        pltpu.make_async_remote_copy(
            src_ref=sq_z.at[src], dst_ref=sq_z.at[src], send_sem=z_ssem.at[o], recv_sem=z_rsem.at[src],
            device_id={"island": base + src}, device_id_type=MESH).wait_recv()
    for cp in z_sends:
        cp.wait_send()
    total = sq_z[0]
    for c in range(1, RING):
        total = total + sq_z[c]
    sq_ref[...] = total


def all_reduce(own, islands, inner):
    halves, rows, cols = own.shape
    chunk = rows // RING
    return pl.pallas_call(
        functools.partial(ring_kernel, islands, inner),
        out_shape=(jax.ShapeDtypeStruct(own.shape, own.dtype), jax.ShapeDtypeStruct((8, 128), jnp.float32)),
        in_specs=[pl.BlockSpec(memory_space=pltpu.VMEM)],
        out_specs=(pl.BlockSpec(memory_space=pltpu.VMEM), pl.BlockSpec(memory_space=pltpu.VMEM)),
        scratch_shapes=[
            pltpu.VMEM((COPIES, halves, chunk, cols), own.dtype),
            pltpu.VMEM((COPIES, halves, chunk, cols), own.dtype),
            pltpu.SemaphoreType.DMA((COPIES,)),
            pltpu.SemaphoreType.DMA((COPIES,)),
            pltpu.VMEM((inner, 8, 128), jnp.float32),
            pltpu.SemaphoreType.DMA((inner,)),
            pltpu.SemaphoreType.DMA((inner,)),
            pltpu.VMEM((RING, 8, 128), jnp.float32),
            pltpu.SemaphoreType.DMA((RING,)),
            pltpu.SemaphoreType.DMA((RING,)),
        ],
        compiler_params=pltpu.CompilerParams(
            collective_id=0, has_side_effects=True, vmem_limit_bytes=48 * 1024 * 1024),
    )(own)


def body(island_delta, params, momentum):
    islands = lax.axis_size("island")
    inner = lax.axis_size("inner")
    count = 2 * D * KVH * HEAD
    average, sq = all_reduce(island_delta[0], islands, inner)
    return outer_update(average, params, momentum, sq[0, 0] / count)


def solution(mesh):
    in_specs = (P("island", None, "inner", None), P(None, "inner", None), P(None, "inner", None))
    out_specs = (P(None, "inner", None), P(None, "inner", None))
    return jax.shard_map(body, mesh=mesh, in_specs=in_specs, out_specs=out_specs, check_vma=False)
```

```python
import functools

import jax
import jax.numpy as jnp
from jax import lax
from jax.experimental import pallas as pl
from jax.experimental.pallas import tpu as pltpu
from jax.sharding import PartitionSpec as P

D = 8192
HEAD = 128
KVH = 4
RING = 8
MESH = pl.DeviceIdType.MESH
PARTS = 4
CHAINS = tuple((d, h, RING // 2 if (d > 0) == (h < PARTS // 2) else (RING - 1) // 2)
               for h in range(PARTS) for d in (1, -1))
RS_BASE = tuple(sum(c[2] for c in CHAINS[:i]) for i in range(len(CHAINS)))
Y = sum(c[2] for c in CHAINS)
AG_BASE = tuple(Y + 1 + base for base in RS_BASE)
COPIES = 2 * Y + 1


def outer_update(average, params, momentum, mean_square):
    factor = jnp.minimum(jnp.float32(1.0), 0.5 / jnp.sqrt(mean_square + 1e-06))
    clipped = factor * average
    new_momentum = 0.9 * momentum + clipped
    new_params = params - 0.7 * (clipped + 0.9 * new_momentum)
    return (new_params, new_momentum)


def ring_kernel(islands, inner, x_ref, out_ref, sq_ref, sbuf, rbuf, ssem, rsem, sq_in, sq_ssem, sq_rsem, sq_z, z_ssem, z_rsem, ybuf):
    chunk = x_ref.shape[1] // RING
    me = lax.axis_index("island")
    col = lax.axis_index("inner")
    z = me % RING
    base = me - z
    right = base + (z + 1) % RING
    left = base + (z + RING - 1) % RING
    partner = (me + RING) % islands

    half = chunk // PARTS

    def rows(k, h=None):
        start = ((z + k + 2 * RING) % RING) * chunk
        if h is None:
            return pl.ds(pl.multiple_of(start, chunk), chunk)
        return pl.ds(pl.multiple_of(start + h * half, half), half)

    def send(k, src, dst, target):
        cp = pltpu.make_async_remote_copy(
            src_ref=src, dst_ref=dst, send_sem=ssem.at[k], recv_sem=rsem.at[k],
            device_id={"island": target}, device_id_type=MESH)
        cp.start()
        return cp

    barrier = pltpu.get_barrier_semaphore()
    for target in (left, right, partner):
        pl.semaphore_signal(barrier, inc=1, device_id={"island": target}, device_id_type=MESH)
    for o in range(1, inner):
        pl.semaphore_signal(barrier, inc=1, device_id={"inner": (col + o) % inner}, device_id_type=MESH)
    for o in range(2, RING - 1):
        pl.semaphore_signal(barrier, inc=1, device_id={"island": base + (z + o) % RING}, device_id_type=MESH)
    pl.semaphore_wait(barrier, 3 + inner - 1 + RING - 3)

    pending = [None] * len(CHAINS)
    for s in range(RING // 2):
        for i, (d, h, r) in enumerate(CHAINS):
            if s >= r:
                continue
            k = RS_BASE[i] + s
            target = right if d > 0 else left
            if s == 0:
                pending[i] = send(k, x_ref.at[:, rows(d * r, h)], rbuf.at[k], target)
                continue
            pending[i].wait()
            sbuf[k] = rbuf[k - 1] + x_ref[:, rows(d * (r - s), h)]
            pending[i] = send(k, sbuf.at[k], rbuf.at[k], target)
    for cp in pending:
        cp.wait()
    for h in range(PARTS):
        own = x_ref[:, rows(0, h)]
        for i, (d, hh, r) in enumerate(CHAINS):
            if hh == h:
                own = own + rbuf[RS_BASE[i] + r - 1]
        ybuf[0, :, pl.ds(h * half, half)] = own
    cy = send(Y, ybuf.at[0], ybuf.at[1], partner)
    cy.wait()
    mine = (ybuf[0] + ybuf[1]) / islands
    out_ref[:, rows(0)] = mine

    sq_in[col] = jnp.full(sq_in.shape[1:], jnp.sum(mine * mine), jnp.float32)
    inner_sends = []
    for o in range(1, inner):
        cp = pltpu.make_async_remote_copy(
            src_ref=sq_in.at[col], dst_ref=sq_in.at[col], send_sem=sq_ssem.at[o], recv_sem=sq_rsem.at[col],
            device_id={"inner": (col + o) % inner}, device_id_type=MESH)
        cp.start()
        inner_sends.append(cp)
    z_sends = []

    def to_z_peers():
        for o in range(1, inner):
            src = (col + inner - o) % inner
            pltpu.make_async_remote_copy(
                src_ref=sq_in.at[src], dst_ref=sq_in.at[src], send_sem=sq_ssem.at[o], recv_sem=sq_rsem.at[src],
                device_id={"inner": src}, device_id_type=MESH).wait_recv()
        for cp in inner_sends:
            cp.wait_send()
        over_inner = sq_in[0]
        for j in range(1, inner):
            over_inner = over_inner + sq_in[j]
        sq_z[z] = over_inner
        for o in range(1, RING):
            cp = pltpu.make_async_remote_copy(
                src_ref=sq_z.at[z], dst_ref=sq_z.at[z], send_sem=z_ssem.at[o], recv_sem=z_rsem.at[z],
                device_id={"island": base + (z + o) % RING}, device_id_type=MESH)
            cp.start()
            z_sends.append(cp)

    for s in range(RING // 2):
        if s == 2:
            to_z_peers()
        for i, (d, h, r) in enumerate(CHAINS):
            if s >= r:
                continue
            if s > 0:
                pending[i].wait()
            k = AG_BASE[i] + s
            place = out_ref.at[:, rows(-d * s, h)]
            pending[i] = send(k, place, place, right if d > 0 else left)
    for cp in pending:
        cp.wait()

    for o in range(1, RING):
        src = (z + RING - o) % RING
        pltpu.make_async_remote_copy(
            src_ref=sq_z.at[src], dst_ref=sq_z.at[src], send_sem=z_ssem.at[o], recv_sem=z_rsem.at[src],
            device_id={"island": base + src}, device_id_type=MESH).wait_recv()
    for cp in z_sends:
        cp.wait_send()
    total = sq_z[0]
    for c in range(1, RING):
        total = total + sq_z[c]
    sq_ref[...] = total


def all_reduce(own, islands, inner):
    halves, rows, cols = own.shape
    chunk = rows // RING
    return pl.pallas_call(
        functools.partial(ring_kernel, islands, inner),
        out_shape=(jax.ShapeDtypeStruct(own.shape, own.dtype), jax.ShapeDtypeStruct((8, 128), jnp.float32)),
        in_specs=[pl.BlockSpec(memory_space=pltpu.VMEM)],
        out_specs=(pl.BlockSpec(memory_space=pltpu.VMEM), pl.BlockSpec(memory_space=pltpu.VMEM)),
        scratch_shapes=[
            pltpu.VMEM((Y, halves, chunk // PARTS, cols), own.dtype),
            pltpu.VMEM((Y, halves, chunk // PARTS, cols), own.dtype),
            pltpu.SemaphoreType.DMA((COPIES,)),
            pltpu.SemaphoreType.DMA((COPIES,)),
            pltpu.VMEM((inner, 8, 128), jnp.float32),
            pltpu.SemaphoreType.DMA((inner,)),
            pltpu.SemaphoreType.DMA((inner,)),
            pltpu.VMEM((RING, 8, 128), jnp.float32),
            pltpu.SemaphoreType.DMA((RING,)),
            pltpu.SemaphoreType.DMA((RING,)),
            pltpu.VMEM((2, halves, chunk, cols), own.dtype),
        ],
        compiler_params=pltpu.CompilerParams(
            collective_id=0, has_side_effects=True, vmem_limit_bytes=48 * 1024 * 1024),
    )(own)


def body(island_delta, params, momentum):
    islands = lax.axis_size("island")
    inner = lax.axis_size("inner")
    count = 2 * D * KVH * HEAD
    average, sq = all_reduce(island_delta[0], islands, inner)
    return outer_update(average, params, momentum, sq[0, 0] / count)


def solution(mesh):
    in_specs = (P("island", None, "inner", None), P(None, "inner", None), P(None, "inner", None))
    out_specs = (P(None, "inner", None), P(None, "inner", None))
    return jax.shard_map(body, mesh=mesh, in_specs=in_specs, out_specs=out_specs, check_vma=False)
```

```python
import functools

import jax
import jax.numpy as jnp
from jax import lax
from jax.experimental import pallas as pl
from jax.experimental.pallas import tpu as pltpu
from jax.sharding import PartitionSpec as P

D = 8192
HEAD = 128
KVH = 4
RING = 8
MESH = pl.DeviceIdType.MESH
PARTS = 4
CHAINS = tuple((d, h, RING // 2 if (d > 0) == (h < PARTS // 2) else (RING - 1) // 2)
               for h in range(PARTS) for d in (1, -1))
RS_BASE = tuple(sum(c[2] for c in CHAINS[:i]) for i in range(len(CHAINS)))
Y = sum(c[2] for c in CHAINS)
AG_BASE = tuple(Y + PARTS + base for base in RS_BASE)
COPIES = 2 * Y + PARTS


def outer_update(average, params, momentum, mean_square):
    factor = jnp.minimum(jnp.float32(1.0), 0.5 / jnp.sqrt(mean_square + 1e-06))
    clipped = factor * average
    new_momentum = 0.9 * momentum + clipped
    new_params = params - 0.7 * (clipped + 0.9 * new_momentum)
    return (new_params, new_momentum)


def ring_kernel(islands, inner, x_ref, out_ref, sq_ref, sbuf, rbuf, ssem, rsem, sq_in, sq_ssem, sq_rsem, sq_z, z_ssem, z_rsem, ybuf):
    chunk = x_ref.shape[1] // RING
    me = lax.axis_index("island")
    col = lax.axis_index("inner")
    z = me % RING
    base = me - z
    right = base + (z + 1) % RING
    left = base + (z + RING - 1) % RING
    partner = (me + RING) % islands

    half = chunk // PARTS

    def rows(k, h=None):
        start = ((z + k + 2 * RING) % RING) * chunk
        if h is None:
            return pl.ds(pl.multiple_of(start, chunk), chunk)
        return pl.ds(pl.multiple_of(start + h * half, half), half)

    def send(k, src, dst, target):
        cp = pltpu.make_async_remote_copy(
            src_ref=src, dst_ref=dst, send_sem=ssem.at[k], recv_sem=rsem.at[k],
            device_id={"island": target}, device_id_type=MESH)
        cp.start()
        return cp

    barrier = pltpu.get_barrier_semaphore()
    for target in (left, right, partner):
        pl.semaphore_signal(barrier, inc=1, device_id={"island": target}, device_id_type=MESH)
    for o in range(1, inner):
        pl.semaphore_signal(barrier, inc=1, device_id={"inner": (col + o) % inner}, device_id_type=MESH)
    for o in range(2, RING - 1):
        pl.semaphore_signal(barrier, inc=1, device_id={"island": base + (z + o) % RING}, device_id_type=MESH)
    pl.semaphore_wait(barrier, 3 + inner - 1 + RING - 3)

    pending = [None] * len(CHAINS)
    for s in range(RING // 2):
        for i, (d, h, r) in enumerate(CHAINS):
            if s >= r:
                continue
            k = RS_BASE[i] + s
            target = right if d > 0 else left
            if s == 0:
                pending[i] = send(k, x_ref.at[:, rows(d * r, h)], rbuf.at[k], target)
                continue
            pending[i].wait()
            sbuf[k] = rbuf[k - 1] + x_ref[:, rows(d * (r - s), h)]
            pending[i] = send(k, sbuf.at[k], rbuf.at[k], target)
    ycopies = []
    for h in range(PARTS):
        own = x_ref[:, rows(0, h)]
        for i, (d, hh, r) in enumerate(CHAINS):
            if hh == h:
                pending[i].wait()
                own = own + rbuf[RS_BASE[i] + r - 1]
        ybuf[0, h] = own
        ycopies.append(send(Y + h, ybuf.at[0, h], ybuf.at[1, h], partner))
    squares = []
    for h in range(PARTS):
        ycopies[h].wait()
        mine = (ybuf[0, h] + ybuf[1, h]) / islands
        out_ref[:, rows(0, h)] = mine
        squares.append(jnp.sum(mine * mine))
        for i, (d, hh, r) in enumerate(CHAINS):
            if hh == h:
                place = out_ref.at[:, rows(0, h)]
                pending[i] = send(AG_BASE[i], place, place, right if d > 0 else left)
    square = squares[0]
    for part in squares[1:]:
        square = square + part

    sq_in[col] = jnp.full(sq_in.shape[1:], square, jnp.float32)
    inner_sends = []
    for o in range(1, inner):
        cp = pltpu.make_async_remote_copy(
            src_ref=sq_in.at[col], dst_ref=sq_in.at[col], send_sem=sq_ssem.at[o], recv_sem=sq_rsem.at[col],
            device_id={"inner": (col + o) % inner}, device_id_type=MESH)
        cp.start()
        inner_sends.append(cp)
    z_sends = []

    def to_z_peers():
        for o in range(1, inner):
            src = (col + inner - o) % inner
            pltpu.make_async_remote_copy(
                src_ref=sq_in.at[src], dst_ref=sq_in.at[src], send_sem=sq_ssem.at[o], recv_sem=sq_rsem.at[src],
                device_id={"inner": src}, device_id_type=MESH).wait_recv()
        for cp in inner_sends:
            cp.wait_send()
        over_inner = sq_in[0]
        for j in range(1, inner):
            over_inner = over_inner + sq_in[j]
        sq_z[z] = over_inner
        for o in range(1, RING):
            cp = pltpu.make_async_remote_copy(
                src_ref=sq_z.at[z], dst_ref=sq_z.at[z], send_sem=z_ssem.at[o], recv_sem=z_rsem.at[z],
                device_id={"island": base + (z + o) % RING}, device_id_type=MESH)
            cp.start()
            z_sends.append(cp)

    for s in range(1, RING // 2):
        if s == 2:
            to_z_peers()
        for i, (d, h, r) in enumerate(CHAINS):
            if s >= r:
                continue
            pending[i].wait()
            k = AG_BASE[i] + s
            place = out_ref.at[:, rows(-d * s, h)]
            pending[i] = send(k, place, place, right if d > 0 else left)
    for cp in pending:
        cp.wait()

    for o in range(1, RING):
        src = (z + RING - o) % RING
        pltpu.make_async_remote_copy(
            src_ref=sq_z.at[src], dst_ref=sq_z.at[src], send_sem=z_ssem.at[o], recv_sem=z_rsem.at[src],
            device_id={"island": base + src}, device_id_type=MESH).wait_recv()
    for cp in z_sends:
        cp.wait_send()
    total = sq_z[0]
    for c in range(1, RING):
        total = total + sq_z[c]
    sq_ref[...] = total


def all_reduce(own, islands, inner):
    halves, rows, cols = own.shape
    chunk = rows // RING
    return pl.pallas_call(
        functools.partial(ring_kernel, islands, inner),
        out_shape=(jax.ShapeDtypeStruct(own.shape, own.dtype), jax.ShapeDtypeStruct((8, 128), jnp.float32)),
        in_specs=[pl.BlockSpec(memory_space=pltpu.VMEM)],
        out_specs=(pl.BlockSpec(memory_space=pltpu.VMEM), pl.BlockSpec(memory_space=pltpu.VMEM)),
        scratch_shapes=[
            pltpu.VMEM((Y, halves, chunk // PARTS, cols), own.dtype),
            pltpu.VMEM((Y, halves, chunk // PARTS, cols), own.dtype),
            pltpu.SemaphoreType.DMA((COPIES,)),
            pltpu.SemaphoreType.DMA((COPIES,)),
            pltpu.VMEM((inner, 8, 128), jnp.float32),
            pltpu.SemaphoreType.DMA((inner,)),
            pltpu.SemaphoreType.DMA((inner,)),
            pltpu.VMEM((RING, 8, 128), jnp.float32),
            pltpu.SemaphoreType.DMA((RING,)),
            pltpu.SemaphoreType.DMA((RING,)),
            pltpu.VMEM((2, PARTS, halves, chunk // PARTS, cols), own.dtype),
        ],
        compiler_params=pltpu.CompilerParams(
            collective_id=0, has_side_effects=True, vmem_limit_bytes=48 * 1024 * 1024),
    )(own)


def body(island_delta, params, momentum):
    islands = lax.axis_size("island")
    inner = lax.axis_size("inner")
    count = 2 * D * KVH * HEAD
    average, sq = all_reduce(island_delta[0], islands, inner)
    return outer_update(average, params, momentum, sq[0, 0] / count)


def solution(mesh):
    in_specs = (P("island", None, "inner", None), P(None, "inner", None), P(None, "inner", None))
    out_specs = (P(None, "inner", None), P(None, "inner", None))
    return jax.shard_map(body, mesh=mesh, in_specs=in_specs, out_specs=out_specs, check_vma=False)
```

```python
import functools

import jax
import jax.numpy as jnp
from jax import lax
from jax.experimental import pallas as pl
from jax.experimental.pallas import tpu as pltpu
from jax.sharding import PartitionSpec as P

D = 8192
HEAD = 128
KVH = 4
RING = 8
MESH = pl.DeviceIdType.MESH
PARTS = 8
CHAINS = tuple((d, h, RING // 2 if (d > 0) == (h < PARTS // 2) else (RING - 1) // 2)
               for h in range(PARTS) for d in (1, -1))
RS_BASE = tuple(sum(c[2] for c in CHAINS[:i]) for i in range(len(CHAINS)))
Y = sum(c[2] for c in CHAINS)
AG_BASE = tuple(Y + PARTS + base for base in RS_BASE)
COPIES = 2 * Y + PARTS


def outer_update(average, params, momentum, mean_square):
    factor = jnp.minimum(jnp.float32(1.0), 0.5 / jnp.sqrt(mean_square + 1e-06))
    clipped = factor * average
    new_momentum = 0.9 * momentum + clipped
    new_params = params - 0.7 * (clipped + 0.9 * new_momentum)
    return (new_params, new_momentum)


def ring_kernel(islands, inner, x_ref, out_ref, sq_ref, sbuf, rbuf, ssem, rsem, sq_in, sq_ssem, sq_rsem, sq_z, z_ssem, z_rsem, ybuf):
    chunk = x_ref.shape[1] // RING
    me = lax.axis_index("island")
    col = lax.axis_index("inner")
    z = me % RING
    base = me - z
    right = base + (z + 1) % RING
    left = base + (z + RING - 1) % RING
    partner = (me + RING) % islands

    half = chunk // PARTS

    def rows(k, h=None):
        start = ((z + k + 2 * RING) % RING) * chunk
        if h is None:
            return pl.ds(pl.multiple_of(start, chunk), chunk)
        return pl.ds(pl.multiple_of(start + h * half, half), half)

    def send(k, src, dst, target):
        cp = pltpu.make_async_remote_copy(
            src_ref=src, dst_ref=dst, send_sem=ssem.at[k], recv_sem=rsem.at[k],
            device_id={"island": target}, device_id_type=MESH)
        cp.start()
        return cp

    barrier = pltpu.get_barrier_semaphore()
    for target in (left, right, partner):
        pl.semaphore_signal(barrier, inc=1, device_id={"island": target}, device_id_type=MESH)
    for o in range(1, inner):
        pl.semaphore_signal(barrier, inc=1, device_id={"inner": (col + o) % inner}, device_id_type=MESH)
    for o in range(2, RING - 1):
        pl.semaphore_signal(barrier, inc=1, device_id={"island": base + (z + o) % RING}, device_id_type=MESH)
    pl.semaphore_wait(barrier, 3 + inner - 1 + RING - 3)

    pending = [None] * len(CHAINS)
    for s in range(RING // 2):
        for i, (d, h, r) in enumerate(CHAINS):
            if s >= r:
                continue
            k = RS_BASE[i] + s
            target = right if d > 0 else left
            if s == 0:
                pending[i] = send(k, x_ref.at[:, rows(d * r, h)], rbuf.at[k], target)
                continue
            pending[i].wait()
            sbuf[k] = rbuf[k - 1] + x_ref[:, rows(d * (r - s), h)]
            pending[i] = send(k, sbuf.at[k], rbuf.at[k], target)
    ycopies = []
    for h in range(PARTS):
        own = x_ref[:, rows(0, h)]
        for i, (d, hh, r) in enumerate(CHAINS):
            if hh == h:
                pending[i].wait()
                own = own + rbuf[RS_BASE[i] + r - 1]
        ybuf[0, h] = own
        ycopies.append(send(Y + h, ybuf.at[0, h], ybuf.at[1, h], partner))
    squares = []
    for h in range(PARTS):
        ycopies[h].wait()
        mine = (ybuf[0, h] + ybuf[1, h]) / islands
        out_ref[:, rows(0, h)] = mine
        squares.append(jnp.sum(mine * mine))
        for i, (d, hh, r) in enumerate(CHAINS):
            if hh == h:
                place = out_ref.at[:, rows(0, h)]
                pending[i] = send(AG_BASE[i], place, place, right if d > 0 else left)
    square = squares[0]
    for part in squares[1:]:
        square = square + part

    sq_in[col] = jnp.full(sq_in.shape[1:], square, jnp.float32)
    inner_sends = []
    for o in range(1, inner):
        cp = pltpu.make_async_remote_copy(
            src_ref=sq_in.at[col], dst_ref=sq_in.at[col], send_sem=sq_ssem.at[o], recv_sem=sq_rsem.at[col],
            device_id={"inner": (col + o) % inner}, device_id_type=MESH)
        cp.start()
        inner_sends.append(cp)
    z_sends = []

    def to_z_peers():
        for o in range(1, inner):
            src = (col + inner - o) % inner
            pltpu.make_async_remote_copy(
                src_ref=sq_in.at[src], dst_ref=sq_in.at[src], send_sem=sq_ssem.at[o], recv_sem=sq_rsem.at[src],
                device_id={"inner": src}, device_id_type=MESH).wait_recv()
        for cp in inner_sends:
            cp.wait_send()
        over_inner = sq_in[0]
        for j in range(1, inner):
            over_inner = over_inner + sq_in[j]
        sq_z[z] = over_inner
        for o in range(1, RING):
            cp = pltpu.make_async_remote_copy(
                src_ref=sq_z.at[z], dst_ref=sq_z.at[z], send_sem=z_ssem.at[o], recv_sem=z_rsem.at[z],
                device_id={"island": base + (z + o) % RING}, device_id_type=MESH)
            cp.start()
            z_sends.append(cp)

    for s in range(1, RING // 2):
        if s == 2:
            to_z_peers()
        for i, (d, h, r) in enumerate(CHAINS):
            if s >= r:
                continue
            pending[i].wait()
            k = AG_BASE[i] + s
            place = out_ref.at[:, rows(-d * s, h)]
            pending[i] = send(k, place, place, right if d > 0 else left)
    for cp in pending:
        cp.wait()

    for o in range(1, RING):
        src = (z + RING - o) % RING
        pltpu.make_async_remote_copy(
            src_ref=sq_z.at[src], dst_ref=sq_z.at[src], send_sem=z_ssem.at[o], recv_sem=z_rsem.at[src],
            device_id={"island": base + src}, device_id_type=MESH).wait_recv()
    for cp in z_sends:
        cp.wait_send()
    total = sq_z[0]
    for c in range(1, RING):
        total = total + sq_z[c]
    sq_ref[...] = total


def all_reduce(own, islands, inner):
    halves, rows, cols = own.shape
    chunk = rows // RING
    return pl.pallas_call(
        functools.partial(ring_kernel, islands, inner),
        out_shape=(jax.ShapeDtypeStruct(own.shape, own.dtype), jax.ShapeDtypeStruct((8, 128), jnp.float32)),
        in_specs=[pl.BlockSpec(memory_space=pltpu.VMEM)],
        out_specs=(pl.BlockSpec(memory_space=pltpu.VMEM), pl.BlockSpec(memory_space=pltpu.VMEM)),
        scratch_shapes=[
            pltpu.VMEM((Y, halves, chunk // PARTS, cols), own.dtype),
            pltpu.VMEM((Y, halves, chunk // PARTS, cols), own.dtype),
            pltpu.SemaphoreType.DMA((COPIES,)),
            pltpu.SemaphoreType.DMA((COPIES,)),
            pltpu.VMEM((inner, 8, 128), jnp.float32),
            pltpu.SemaphoreType.DMA((inner,)),
            pltpu.SemaphoreType.DMA((inner,)),
            pltpu.VMEM((RING, 8, 128), jnp.float32),
            pltpu.SemaphoreType.DMA((RING,)),
            pltpu.SemaphoreType.DMA((RING,)),
            pltpu.VMEM((2, PARTS, halves, chunk // PARTS, cols), own.dtype),
        ],
        compiler_params=pltpu.CompilerParams(
            collective_id=0, has_side_effects=True, vmem_limit_bytes=48 * 1024 * 1024),
    )(own)


def body(island_delta, params, momentum):
    islands = lax.axis_size("island")
    inner = lax.axis_size("inner")
    count = 2 * D * KVH * HEAD
    average, sq = all_reduce(island_delta[0], islands, inner)
    return outer_update(average, params, momentum, sq[0, 0] / count)


def solution(mesh):
    in_specs = (P("island", None, "inner", None), P(None, "inner", None), P(None, "inner", None))
    out_specs = (P(None, "inner", None), P(None, "inner", None))
    return jax.shard_map(body, mesh=mesh, in_specs=in_specs, out_specs=out_specs, check_vma=False)
```

```python
import functools

import jax
import jax.numpy as jnp
from jax import lax
from jax.experimental import pallas as pl
from jax.experimental.pallas import tpu as pltpu
from jax.sharding import PartitionSpec as P

D = 8192
HEAD = 128
KVH = 4
RING = 8
MESH = pl.DeviceIdType.MESH
PARTS = 8
CHAINS = tuple((d, h, RING // 2 if (d > 0) == (h < PARTS // 2) else (RING - 1) // 2)
               for h in range(PARTS) for d in (1, -1))
RS_BASE = tuple(sum(c[2] for c in CHAINS[:i]) for i in range(len(CHAINS)))
Y = sum(c[2] for c in CHAINS)
AG_BASE = tuple(Y + PARTS + base for base in RS_BASE)
COPIES = 2 * Y + PARTS


def outer_update(average, params, momentum, mean_square):
    factor = jnp.minimum(jnp.float32(1.0), 0.5 / jnp.sqrt(mean_square + 1e-06))
    clipped = factor * average
    new_momentum = 0.9 * momentum + clipped
    new_params = params - 0.7 * (clipped + 0.9 * new_momentum)
    return (new_params, new_momentum)


def ring_kernel(islands, inner, x_hbm, out_ref, sq_ref, sbuf, rbuf, ssem, rsem, sq_in, sq_ssem, sq_rsem, sq_z, z_ssem, z_rsem, ybuf, x_ref, x_sem):
    chunk = x_hbm.shape[1] // RING
    me = lax.axis_index("island")
    col = lax.axis_index("inner")
    z = me % RING
    base = me - z
    right = base + (z + 1) % RING
    left = base + (z + RING - 1) % RING
    partner = (me + RING) % islands

    half = chunk // PARTS

    def rows(k, h=None):
        start = ((z + k + 2 * RING) % RING) * chunk
        if h is None:
            return pl.ds(pl.multiple_of(start, chunk), chunk)
        return pl.ds(pl.multiple_of(start + h * half, half), half)

    def send(k, src, dst, target):
        cp = pltpu.make_async_remote_copy(
            src_ref=src, dst_ref=dst, send_sem=ssem.at[k], recv_sem=rsem.at[k],
            device_id={"island": target}, device_id_type=MESH)
        cp.start()
        return cp

    load = pltpu.make_async_copy(x_hbm, x_ref, x_sem)
    load.start()
    barrier = pltpu.get_barrier_semaphore()
    for target in (left, right, partner):
        pl.semaphore_signal(barrier, inc=1, device_id={"island": target}, device_id_type=MESH)
    for o in range(1, inner):
        pl.semaphore_signal(barrier, inc=1, device_id={"inner": (col + o) % inner}, device_id_type=MESH)
    for o in range(2, RING - 1):
        pl.semaphore_signal(barrier, inc=1, device_id={"island": base + (z + o) % RING}, device_id_type=MESH)
    pl.semaphore_wait(barrier, 3 + inner - 1 + RING - 3)

    pending = [None] * len(CHAINS)
    for s in range(RING // 2):
        for i, (d, h, r) in enumerate(CHAINS):
            if s >= r:
                continue
            k = RS_BASE[i] + s
            target = right if d > 0 else left
            if s == 0:
                pending[i] = send(k, x_hbm.at[:, rows(d * r, h)], rbuf.at[k], target)
                continue
            if s == 1 and i == 0:
                load.wait()
            pending[i].wait()
            sbuf[k] = rbuf[k - 1] + x_ref[:, rows(d * (r - s), h)]
            pending[i] = send(k, sbuf.at[k], rbuf.at[k], target)
    ycopies = []
    for h in range(PARTS):
        own = x_ref[:, rows(0, h)]
        for i, (d, hh, r) in enumerate(CHAINS):
            if hh == h:
                pending[i].wait()
                own = own + rbuf[RS_BASE[i] + r - 1]
        ybuf[0, h] = own
        ycopies.append(send(Y + h, ybuf.at[0, h], ybuf.at[1, h], partner))
    squares = []
    for h in range(PARTS):
        ycopies[h].wait()
        mine = (ybuf[0, h] + ybuf[1, h]) / islands
        out_ref[:, rows(0, h)] = mine
        squares.append(jnp.sum(mine * mine))
        for i, (d, hh, r) in enumerate(CHAINS):
            if hh == h:
                place = out_ref.at[:, rows(0, h)]
                pending[i] = send(AG_BASE[i], place, place, right if d > 0 else left)
    square = squares[0]
    for part in squares[1:]:
        square = square + part

    sq_in[col] = jnp.full(sq_in.shape[1:], square, jnp.float32)
    inner_sends = []
    for o in range(1, inner):
        cp = pltpu.make_async_remote_copy(
            src_ref=sq_in.at[col], dst_ref=sq_in.at[col], send_sem=sq_ssem.at[o], recv_sem=sq_rsem.at[col],
            device_id={"inner": (col + o) % inner}, device_id_type=MESH)
        cp.start()
        inner_sends.append(cp)
    z_sends = []

    def to_z_peers():
        for o in range(1, inner):
            src = (col + inner - o) % inner
            pltpu.make_async_remote_copy(
                src_ref=sq_in.at[src], dst_ref=sq_in.at[src], send_sem=sq_ssem.at[o], recv_sem=sq_rsem.at[src],
                device_id={"inner": src}, device_id_type=MESH).wait_recv()
        for cp in inner_sends:
            cp.wait_send()
        over_inner = sq_in[0]
        for j in range(1, inner):
            over_inner = over_inner + sq_in[j]
        sq_z[z] = over_inner
        for o in range(1, RING):
            cp = pltpu.make_async_remote_copy(
                src_ref=sq_z.at[z], dst_ref=sq_z.at[z], send_sem=z_ssem.at[o], recv_sem=z_rsem.at[z],
                device_id={"island": base + (z + o) % RING}, device_id_type=MESH)
            cp.start()
            z_sends.append(cp)

    for s in range(1, RING // 2):
        if s == 2:
            to_z_peers()
        for i, (d, h, r) in enumerate(CHAINS):
            if s >= r:
                continue
            pending[i].wait()
            k = AG_BASE[i] + s
            place = out_ref.at[:, rows(-d * s, h)]
            pending[i] = send(k, place, place, right if d > 0 else left)
    for cp in pending:
        cp.wait()

    for o in range(1, RING):
        src = (z + RING - o) % RING
        pltpu.make_async_remote_copy(
            src_ref=sq_z.at[src], dst_ref=sq_z.at[src], send_sem=z_ssem.at[o], recv_sem=z_rsem.at[src],
            device_id={"island": base + src}, device_id_type=MESH).wait_recv()
    for cp in z_sends:
        cp.wait_send()
    total = sq_z[0]
    for c in range(1, RING):
        total = total + sq_z[c]
    sq_ref[...] = total


def all_reduce(own, islands, inner):
    halves, rows, cols = own.shape
    chunk = rows // RING
    return pl.pallas_call(
        functools.partial(ring_kernel, islands, inner),
        out_shape=(jax.ShapeDtypeStruct(own.shape, own.dtype), jax.ShapeDtypeStruct((8, 128), jnp.float32)),
        in_specs=[pl.BlockSpec(memory_space=pl.ANY)],
        out_specs=(pl.BlockSpec(memory_space=pltpu.VMEM), pl.BlockSpec(memory_space=pltpu.VMEM)),
        scratch_shapes=[
            pltpu.VMEM((Y, halves, chunk // PARTS, cols), own.dtype),
            pltpu.VMEM((Y, halves, chunk // PARTS, cols), own.dtype),
            pltpu.SemaphoreType.DMA((COPIES,)),
            pltpu.SemaphoreType.DMA((COPIES,)),
            pltpu.VMEM((inner, 8, 128), jnp.float32),
            pltpu.SemaphoreType.DMA((inner,)),
            pltpu.SemaphoreType.DMA((inner,)),
            pltpu.VMEM((RING, 8, 128), jnp.float32),
            pltpu.SemaphoreType.DMA((RING,)),
            pltpu.SemaphoreType.DMA((RING,)),
            pltpu.VMEM((2, PARTS, halves, chunk // PARTS, cols), own.dtype),
            pltpu.VMEM(own.shape, own.dtype),
            pltpu.SemaphoreType.DMA(()),
        ],
        compiler_params=pltpu.CompilerParams(
            collective_id=0, has_side_effects=True, vmem_limit_bytes=67043328),
    )(own)


def body(island_delta, params, momentum):
    islands = lax.axis_size("island")
    inner = lax.axis_size("inner")
    count = 2 * D * KVH * HEAD
    average, sq = all_reduce(island_delta[0], islands, inner)
    return outer_update(average, params, momentum, sq[0, 0] / count)


def solution(mesh):
    in_specs = (P("island", None, "inner", None), P(None, "inner", None), P(None, "inner", None))
    out_specs = (P(None, "inner", None), P(None, "inner", None))
    return jax.shard_map(body, mesh=mesh, in_specs=in_specs, out_specs=out_specs, check_vma=False)
```

```python
import functools

import jax
import jax.numpy as jnp
from jax import lax
from jax.experimental import pallas as pl
from jax.experimental.pallas import tpu as pltpu
from jax.sharding import PartitionSpec as P

D = 8192
HEAD = 128
KVH = 4
RING = 8
MESH = pl.DeviceIdType.MESH
PARTS = 8
CHAINS = tuple((d, h, RING // 2 if (d > 0) == (h < PARTS // 2) else (RING - 1) // 2)
               for h in range(PARTS) for d in (1, -1))
RS_BASE = tuple(sum(c[2] for c in CHAINS[:i]) for i in range(len(CHAINS)))
Y = sum(c[2] for c in CHAINS)
AG_BASE = tuple(Y + PARTS + base for base in RS_BASE)
COPIES = 2 * Y + PARTS


def outer_update(average, params, momentum, mean_square):
    factor = jnp.minimum(jnp.float32(1.0), 0.5 / jnp.sqrt(mean_square + 1e-06))
    clipped = factor * average
    new_momentum = 0.9 * momentum + clipped
    new_params = params - 0.7 * (clipped + 0.9 * new_momentum)
    return (new_params, new_momentum)


def ring_kernel(islands, inner, x_ref, out_ref, sq_ref, sbuf, rbuf, ssem, rsem, sq_in, sq_ssem, sq_rsem, sq_z, z_ssem, z_rsem, ybuf):
    chunk = x_ref.shape[1] // RING
    me = lax.axis_index("island")
    col = lax.axis_index("inner")
    z = me % RING
    base = me - z
    right = base + (z + 1) % RING
    left = base + (z + RING - 1) % RING
    partner = (me + RING) % islands

    half = chunk // PARTS

    def rows(k, h=None):
        start = ((z + k + 2 * RING) % RING) * chunk
        if h is None:
            return pl.ds(pl.multiple_of(start, chunk), chunk)
        return pl.ds(pl.multiple_of(start + h * half, half), half)

    def send(k, src, dst, target):
        cp = pltpu.make_async_remote_copy(
            src_ref=src, dst_ref=dst, send_sem=ssem.at[k], recv_sem=rsem.at[k],
            device_id={"island": target}, device_id_type=MESH)
        cp.start()
        return cp

    barrier = pltpu.get_barrier_semaphore()
    for target in (left, right, partner):
        pl.semaphore_signal(barrier, inc=1, device_id={"island": target}, device_id_type=MESH)
    for o in range(1, inner):
        pl.semaphore_signal(barrier, inc=1, device_id={"inner": (col + o) % inner}, device_id_type=MESH)
    for o in range(2, RING - 1):
        pl.semaphore_signal(barrier, inc=1, device_id={"island": base + (z + o) % RING}, device_id_type=MESH)
    pl.semaphore_wait(barrier, 3 + inner - 1 + RING - 3)

    pending = [None] * len(CHAINS)
    for s in range(RING // 2):
        for i, (d, h, r) in enumerate(CHAINS):
            if s >= r:
                continue
            k = RS_BASE[i] + s
            target = right if d > 0 else left
            if s == 0:
                pending[i] = send(k, x_ref.at[:, rows(d * r, h)], rbuf.at[k], target)
                continue
            pending[i].wait()
            sbuf[k] = rbuf[k - 1] + x_ref[:, rows(d * (r - s), h)]
            pending[i] = send(k, sbuf.at[k], rbuf.at[k], target)
    ycopies = []
    for h in range(PARTS):
        own = x_ref[:, rows(0, h)]
        for i, (d, hh, r) in enumerate(CHAINS):
            if hh == h:
                pending[i].wait()
                own = own + rbuf[RS_BASE[i] + r - 1]
        ybuf[0, h] = own
        ycopies.append(send(Y + h, ybuf.at[0, h], ybuf.at[1, h], partner))
    squares = []
    for h in range(PARTS):
        ycopies[h].wait()
        mine = (ybuf[0, h] + ybuf[1, h]) / islands
        out_ref[:, rows(0, h)] = mine
        squares.append(jnp.sum(mine * mine))
        for i, (d, hh, r) in enumerate(CHAINS):
            if hh == h:
                place = out_ref.at[:, rows(0, h)]
                pending[i] = send(AG_BASE[i], place, place, right if d > 0 else left)
    square = squares[0]
    for part in squares[1:]:
        square = square + part

    sq_in[col] = jnp.full(sq_in.shape[1:], square, jnp.float32)
    inner_sends = []
    for o in range(1, inner):
        cp = pltpu.make_async_remote_copy(
            src_ref=sq_in.at[col], dst_ref=sq_in.at[col], send_sem=sq_ssem.at[o], recv_sem=sq_rsem.at[col],
            device_id={"inner": (col + o) % inner}, device_id_type=MESH)
        cp.start()
        inner_sends.append(cp)
    z_sends = []

    def to_z_peers():
        for o in range(1, inner):
            src = (col + inner - o) % inner
            pltpu.make_async_remote_copy(
                src_ref=sq_in.at[src], dst_ref=sq_in.at[src], send_sem=sq_ssem.at[o], recv_sem=sq_rsem.at[src],
                device_id={"inner": src}, device_id_type=MESH).wait_recv()
        for cp in inner_sends:
            cp.wait_send()
        over_inner = sq_in[0]
        for j in range(1, inner):
            over_inner = over_inner + sq_in[j]
        sq_z[z] = over_inner
        for o in range(1, RING):
            cp = pltpu.make_async_remote_copy(
                src_ref=sq_z.at[z], dst_ref=sq_z.at[z], send_sem=z_ssem.at[o], recv_sem=z_rsem.at[z],
                device_id={"island": base + (z + o) % RING}, device_id_type=MESH)
            cp.start()
            z_sends.append(cp)

    for s in range(1, RING // 2):
        if s == 2:
            to_z_peers()
        for i, (d, h, r) in enumerate(CHAINS):
            if s >= r:
                continue
            pending[i].wait()
            k = AG_BASE[i] + s
            place = out_ref.at[:, rows(-d * s, h)]
            pending[i] = send(k, place, place, right if d > 0 else left)
    for cp in pending:
        cp.wait()

    for o in range(1, RING):
        src = (z + RING - o) % RING
        pltpu.make_async_remote_copy(
            src_ref=sq_z.at[src], dst_ref=sq_z.at[src], send_sem=z_ssem.at[o], recv_sem=z_rsem.at[src],
            device_id={"island": base + src}, device_id_type=MESH).wait_recv()
    for cp in z_sends:
        cp.wait_send()
    total = sq_z[0]
    for c in range(1, RING):
        total = total + sq_z[c]
    sq_ref[...] = total[0:1, 0:1]


def all_reduce(own, islands, inner):
    halves, rows, cols = own.shape
    chunk = rows // RING
    return pl.pallas_call(
        functools.partial(ring_kernel, islands, inner),
        out_shape=(jax.ShapeDtypeStruct(own.shape, own.dtype), jax.ShapeDtypeStruct((1, 1), jnp.float32)),
        in_specs=[pl.BlockSpec(memory_space=pltpu.VMEM)],
        out_specs=(pl.BlockSpec(memory_space=pltpu.VMEM), pl.BlockSpec(memory_space=pltpu.VMEM)),
        scratch_shapes=[
            pltpu.VMEM((Y, halves, chunk // PARTS, cols), own.dtype),
            pltpu.VMEM((Y, halves, chunk // PARTS, cols), own.dtype),
            pltpu.SemaphoreType.DMA((COPIES,)),
            pltpu.SemaphoreType.DMA((COPIES,)),
            pltpu.VMEM((inner, 8, 128), jnp.float32),
            pltpu.SemaphoreType.DMA((inner,)),
            pltpu.SemaphoreType.DMA((inner,)),
            pltpu.VMEM((RING, 8, 128), jnp.float32),
            pltpu.SemaphoreType.DMA((RING,)),
            pltpu.SemaphoreType.DMA((RING,)),
            pltpu.VMEM((2, PARTS, halves, chunk // PARTS, cols), own.dtype),
        ],
        compiler_params=pltpu.CompilerParams(
            collective_id=0, has_side_effects=True, vmem_limit_bytes=48 * 1024 * 1024),
    )(own)


def body(island_delta, params, momentum):
    islands = lax.axis_size("island")
    inner = lax.axis_size("inner")
    count = 2 * D * KVH * HEAD
    average, sq = all_reduce(island_delta[0], islands, inner)
    return outer_update(average, params, momentum, sq.reshape(()) / count)


def solution(mesh):
    in_specs = (P("island", None, "inner", None), P(None, "inner", None), P(None, "inner", None))
    out_specs = (P(None, "inner", None), P(None, "inner", None))
    return jax.shard_map(body, mesh=mesh, in_specs=in_specs, out_specs=out_specs, check_vma=False)
```

```python
import functools

import jax
import jax.numpy as jnp
from jax import lax
from jax.experimental import pallas as pl
from jax.experimental.pallas import tpu as pltpu
from jax.sharding import PartitionSpec as P

D = 8192
HEAD = 128
KVH = 4
RING = 8
MESH = pl.DeviceIdType.MESH
PARTS = 8
CHAINS = tuple((d, h, RING // 2 if (d > 0) == (h < PARTS // 2) else (RING - 1) // 2)
               for h in range(PARTS) for d in (1, -1))
RS_BASE = tuple(sum(c[2] for c in CHAINS[:i]) for i in range(len(CHAINS)))
Y = sum(c[2] for c in CHAINS)
AG_BASE = tuple(Y + PARTS + base for base in RS_BASE)
COPIES = 2 * Y + PARTS


def outer_update(average, params, momentum, mean_square):
    factor = jnp.minimum(jnp.float32(1.0), 0.5 / jnp.sqrt(mean_square + 1e-06))
    clipped = factor * average
    new_momentum = 0.9 * momentum + clipped
    new_params = params - 0.7 * (clipped + 0.9 * new_momentum)
    return (new_params, new_momentum)


def ring_kernel(islands, inner, x_ref, out_ref, sq_ref, sbuf, rbuf, ssem, rsem, sq_in, sq_ssem, sq_rsem, sq_z, z_ssem, z_rsem, ybuf):
    chunk = x_ref.shape[1] // RING
    me = lax.axis_index("island")
    col = lax.axis_index("inner")
    z = me % RING
    base = me - z
    right = base + (z + 1) % RING
    left = base + (z + RING - 1) % RING
    partner = (me + RING) % islands

    half = chunk // PARTS

    def rows(k, h=None):
        start = ((z + k + 2 * RING) % RING) * chunk
        if h is None:
            return pl.ds(pl.multiple_of(start, chunk), chunk)
        return pl.ds(pl.multiple_of(start + h * half, half), half)

    def send(k, src, dst, target):
        cp = pltpu.make_async_remote_copy(
            src_ref=src, dst_ref=dst, send_sem=ssem.at[k], recv_sem=rsem.at[k],
            device_id={"island": target}, device_id_type=MESH)
        cp.start()
        return cp

    barrier = pltpu.get_barrier_semaphore()
    for target in (left, right, partner):
        pl.semaphore_signal(barrier, inc=1, device_id={"island": target}, device_id_type=MESH)
    for o in range(1, inner):
        pl.semaphore_signal(barrier, inc=1, device_id={"inner": (col + o) % inner}, device_id_type=MESH)
    for o in range(2, RING - 1):
        pl.semaphore_signal(barrier, inc=1, device_id={"island": base + (z + o) % RING}, device_id_type=MESH)
    pl.semaphore_wait(barrier, 3 + inner - 1 + RING - 3)

    pending = [None] * len(CHAINS)
    for s in range(RING // 2):
        for i, (d, h, r) in enumerate(CHAINS):
            if s >= r:
                continue
            k = RS_BASE[i] + s
            target = right if d > 0 else left
            if s == 0:
                pending[i] = send(k, x_ref.at[:, rows(d * r, h)], rbuf.at[k], target)
                continue
            pending[i].wait()
            sbuf[k] = rbuf[k - 1] + x_ref[:, rows(d * (r - s), h)]
            pending[i] = send(k, sbuf.at[k], rbuf.at[k], target)
    ycopies = []
    for h in range(PARTS):
        own = x_ref[:, rows(0, h)]
        for i, (d, hh, r) in enumerate(CHAINS):
            if hh == h:
                pending[i].wait()
                own = own + rbuf[RS_BASE[i] + r - 1]
        ybuf[0, h] = own
        ycopies.append(send(Y + h, ybuf.at[0, h], ybuf.at[1, h], partner))
    squares = []
    for h in range(PARTS):
        ycopies[h].wait()
        mine = (ybuf[0, h] + ybuf[1, h]) / islands
        out_ref[:, rows(0, h)] = mine
        squares.append(jnp.sum(mine * mine))
        for i, (d, hh, r) in enumerate(CHAINS):
            if hh == h:
                place = out_ref.at[:, rows(0, h)]
                pending[i] = send(AG_BASE[i], place, place, right if d > 0 else left)
    square = squares[0]
    for part in squares[1:]:
        square = square + part

    sq_in[col] = jnp.full(sq_in.shape[1:], square, jnp.float32)
    inner_sends = []
    for o in range(1, inner):
        cp = pltpu.make_async_remote_copy(
            src_ref=sq_in.at[col], dst_ref=sq_in.at[col], send_sem=sq_ssem.at[o], recv_sem=sq_rsem.at[col],
            device_id={"inner": (col + o) % inner}, device_id_type=MESH)
        cp.start()
        inner_sends.append(cp)
    z_sends = []

    def to_z_peers():
        for o in range(1, inner):
            src = (col + inner - o) % inner
            pltpu.make_async_remote_copy(
                src_ref=sq_in.at[src], dst_ref=sq_in.at[src], send_sem=sq_ssem.at[o], recv_sem=sq_rsem.at[src],
                device_id={"inner": src}, device_id_type=MESH).wait_recv()
        for cp in inner_sends:
            cp.wait_send()
        over_inner = sq_in[0]
        for j in range(1, inner):
            over_inner = over_inner + sq_in[j]
        sq_z[z] = over_inner
        for o in range(1, RING):
            cp = pltpu.make_async_remote_copy(
                src_ref=sq_z.at[z], dst_ref=sq_z.at[z], send_sem=z_ssem.at[o], recv_sem=z_rsem.at[z],
                device_id={"island": base + (z + o) % RING}, device_id_type=MESH)
            cp.start()
            z_sends.append(cp)

    for s in range(1, RING // 2):
        if s == 1:
            to_z_peers()
        for i, (d, h, r) in enumerate(CHAINS):
            if s >= r:
                continue
            pending[i].wait()
            k = AG_BASE[i] + s
            place = out_ref.at[:, rows(-d * s, h)]
            pending[i] = send(k, place, place, right if d > 0 else left)
    for cp in pending:
        cp.wait()

    for o in range(1, RING):
        src = (z + RING - o) % RING
        pltpu.make_async_remote_copy(
            src_ref=sq_z.at[src], dst_ref=sq_z.at[src], send_sem=z_ssem.at[o], recv_sem=z_rsem.at[src],
            device_id={"island": base + src}, device_id_type=MESH).wait_recv()
    for cp in z_sends:
        cp.wait_send()
    total = sq_z[0]
    for c in range(1, RING):
        total = total + sq_z[c]
    sq_ref[...] = total


def all_reduce(own, islands, inner):
    halves, rows, cols = own.shape
    chunk = rows // RING
    return pl.pallas_call(
        functools.partial(ring_kernel, islands, inner),
        out_shape=(jax.ShapeDtypeStruct(own.shape, own.dtype), jax.ShapeDtypeStruct((8, 128), jnp.float32)),
        in_specs=[pl.BlockSpec(memory_space=pltpu.VMEM)],
        out_specs=(pl.BlockSpec(memory_space=pltpu.VMEM), pl.BlockSpec(memory_space=pltpu.VMEM)),
        scratch_shapes=[
            pltpu.VMEM((Y, halves, chunk // PARTS, cols), own.dtype),
            pltpu.VMEM((Y, halves, chunk // PARTS, cols), own.dtype),
            pltpu.SemaphoreType.DMA((COPIES,)),
            pltpu.SemaphoreType.DMA((COPIES,)),
            pltpu.VMEM((inner, 8, 128), jnp.float32),
            pltpu.SemaphoreType.DMA((inner,)),
            pltpu.SemaphoreType.DMA((inner,)),
            pltpu.VMEM((RING, 8, 128), jnp.float32),
            pltpu.SemaphoreType.DMA((RING,)),
            pltpu.SemaphoreType.DMA((RING,)),
            pltpu.VMEM((2, PARTS, halves, chunk // PARTS, cols), own.dtype),
        ],
        compiler_params=pltpu.CompilerParams(
            collective_id=0, has_side_effects=True, vmem_limit_bytes=48 * 1024 * 1024),
    )(own)


def body(island_delta, params, momentum):
    islands = lax.axis_size("island")
    inner = lax.axis_size("inner")
    count = 2 * D * KVH * HEAD
    average, sq = all_reduce(island_delta[0], islands, inner)
    return outer_update(average, params, momentum, sq[0, 0] / count)


def solution(mesh):
    in_specs = (P("island", None, "inner", None), P(None, "inner", None), P(None, "inner", None))
    out_specs = (P(None, "inner", None), P(None, "inner", None))
    return jax.shard_map(body, mesh=mesh, in_specs=in_specs, out_specs=out_specs, check_vma=False)
```

```python
import functools

import jax
import jax.numpy as jnp
from jax import lax
from jax.experimental import pallas as pl
from jax.experimental.pallas import tpu as pltpu
from jax.sharding import PartitionSpec as P

D = 8192
HEAD = 128
KVH = 4
RING = 8
MESH = pl.DeviceIdType.MESH
PARTS = 8
CHAINS = tuple((d, h, RING // 2 if (d > 0) == (h < PARTS // 2) else (RING - 1) // 2)
               for h in range(PARTS) for d in (1, -1))
RS_BASE = tuple(sum(c[2] for c in CHAINS[:i]) for i in range(len(CHAINS)))
Y = sum(c[2] for c in CHAINS)
AG_BASE = tuple(Y + PARTS + base for base in RS_BASE)
COPIES = 2 * Y + PARTS


def outer_update(average, params, momentum, mean_square):
    factor = jnp.minimum(jnp.float32(1.0), 0.5 / jnp.sqrt(mean_square + 1e-06))
    clipped = factor * average
    new_momentum = 0.9 * momentum + clipped
    new_params = params - 0.7 * (clipped + 0.9 * new_momentum)
    return (new_params, new_momentum)


def ring_kernel(islands, inner, x_ref, out_ref, sq_ref, sbuf, rbuf, ssem, rsem, sq_in, sq_ssem, sq_rsem, sq_z, z_ssem, z_rsem, ybuf):
    chunk = x_ref.shape[1] // RING
    me = lax.axis_index("island")
    col = lax.axis_index("inner")
    z = me % RING
    base = me - z
    right = base + (z + 1) % RING
    left = base + (z + RING - 1) % RING
    partner = (me + RING) % islands

    half = chunk // PARTS

    def rows(k, h=None):
        start = ((z + k + 2 * RING) % RING) * chunk
        if h is None:
            return pl.ds(pl.multiple_of(start, chunk), chunk)
        return pl.ds(pl.multiple_of(start + h * half, half), half)

    def send(k, src, dst, target):
        cp = pltpu.make_async_remote_copy(
            src_ref=src, dst_ref=dst, send_sem=ssem.at[k], recv_sem=rsem.at[k],
            device_id={"island": target}, device_id_type=MESH)
        cp.start()
        return cp

    barrier = pltpu.get_barrier_semaphore()
    for target in (left, right, partner):
        pl.semaphore_signal(barrier, inc=1, device_id={"island": target}, device_id_type=MESH)
    for o in range(1, inner):
        pl.semaphore_signal(barrier, inc=1, device_id={"inner": (col + o) % inner}, device_id_type=MESH)
    for o in range(2, RING - 1):
        pl.semaphore_signal(barrier, inc=1, device_id={"island": base + (z + o) % RING}, device_id_type=MESH)
    pl.semaphore_wait(barrier, 3 + inner - 1 + RING - 3)

    pending = [None] * len(CHAINS)
    for s in range(RING // 2):
        for i, (d, h, r) in enumerate(CHAINS):
            if s >= r:
                continue
            k = RS_BASE[i] + s
            target = right if d > 0 else left
            if s == 0:
                pending[i] = send(k, x_ref.at[:, rows(d * r, h)], rbuf.at[k], target)
                continue
            pending[i].wait()
            sbuf[k] = rbuf[k - 1] + x_ref[:, rows(d * (r - s), h)]
            pending[i] = send(k, sbuf.at[k], rbuf.at[k], target)
    ycopies = []
    for h in range(PARTS):
        own = x_ref[:, rows(0, h)]
        for i, (d, hh, r) in enumerate(CHAINS):
            if hh == h:
                pending[i].wait()
                own = own + rbuf[RS_BASE[i] + r - 1]
        ybuf[0, h] = own
        ycopies.append(send(Y + h, ybuf.at[0, h], ybuf.at[1, h], partner))
    squares = []
    for h in range(PARTS):
        ycopies[h].wait()
        mine = (ybuf[0, h] + ybuf[1, h]) / islands
        out_ref[:, rows(0, h)] = mine
        squares.append(jnp.sum(mine * mine))
        for i, (d, hh, r) in enumerate(CHAINS):
            if hh == h:
                place = out_ref.at[:, rows(0, h)]
                pending[i] = send(AG_BASE[i], place, place, right if d > 0 else left)
    square = squares[0]
    for part in squares[1:]:
        square = square + part

    sq_in[col] = jnp.full(sq_in.shape[1:], square, jnp.float32)
    inner_sends = []
    for o in range(1, inner):
        cp = pltpu.make_async_remote_copy(
            src_ref=sq_in.at[col], dst_ref=sq_in.at[col], send_sem=sq_ssem.at[o], recv_sem=sq_rsem.at[col],
            device_id={"inner": (col + o) % inner}, device_id_type=MESH)
        cp.start()
        inner_sends.append(cp)
    z_sends = []

    def to_z_peers():
        for o in range(1, inner):
            src = (col + inner - o) % inner
            pltpu.make_async_remote_copy(
                src_ref=sq_in.at[src], dst_ref=sq_in.at[src], send_sem=sq_ssem.at[o], recv_sem=sq_rsem.at[src],
                device_id={"inner": src}, device_id_type=MESH).wait_recv()
        for cp in inner_sends:
            cp.wait_send()
        over_inner = sq_in[0]
        for j in range(1, inner):
            over_inner = over_inner + sq_in[j]
        sq_z[z] = over_inner
        for o in range(1, RING):
            cp = pltpu.make_async_remote_copy(
                src_ref=sq_z.at[z], dst_ref=sq_z.at[z], send_sem=z_ssem.at[o], recv_sem=z_rsem.at[z],
                device_id={"island": base + (z + o) % RING}, device_id_type=MESH)
            cp.start()
            z_sends.append(cp)

    for s in range(1, RING // 2):
        if s == 3:
            to_z_peers()
        for i, (d, h, r) in enumerate(CHAINS):
            if s >= r:
                continue
            pending[i].wait()
            k = AG_BASE[i] + s
            place = out_ref.at[:, rows(-d * s, h)]
            pending[i] = send(k, place, place, right if d > 0 else left)
    for cp in pending:
        cp.wait()

    for o in range(1, RING):
        src = (z + RING - o) % RING
        pltpu.make_async_remote_copy(
            src_ref=sq_z.at[src], dst_ref=sq_z.at[src], send_sem=z_ssem.at[o], recv_sem=z_rsem.at[src],
            device_id={"island": base + src}, device_id_type=MESH).wait_recv()
    for cp in z_sends:
        cp.wait_send()
    total = sq_z[0]
    for c in range(1, RING):
        total = total + sq_z[c]
    sq_ref[...] = total


def all_reduce(own, islands, inner):
    halves, rows, cols = own.shape
    chunk = rows // RING
    return pl.pallas_call(
        functools.partial(ring_kernel, islands, inner),
        out_shape=(jax.ShapeDtypeStruct(own.shape, own.dtype), jax.ShapeDtypeStruct((8, 128), jnp.float32)),
        in_specs=[pl.BlockSpec(memory_space=pltpu.VMEM)],
        out_specs=(pl.BlockSpec(memory_space=pltpu.VMEM), pl.BlockSpec(memory_space=pltpu.VMEM)),
        scratch_shapes=[
            pltpu.VMEM((Y, halves, chunk // PARTS, cols), own.dtype),
            pltpu.VMEM((Y, halves, chunk // PARTS, cols), own.dtype),
            pltpu.SemaphoreType.DMA((COPIES,)),
            pltpu.SemaphoreType.DMA((COPIES,)),
            pltpu.VMEM((inner, 8, 128), jnp.float32),
            pltpu.SemaphoreType.DMA((inner,)),
            pltpu.SemaphoreType.DMA((inner,)),
            pltpu.VMEM((RING, 8, 128), jnp.float32),
            pltpu.SemaphoreType.DMA((RING,)),
            pltpu.SemaphoreType.DMA((RING,)),
            pltpu.VMEM((2, PARTS, halves, chunk // PARTS, cols), own.dtype),
        ],
        compiler_params=pltpu.CompilerParams(
            collective_id=0, has_side_effects=True, vmem_limit_bytes=48 * 1024 * 1024),
    )(own)


def body(island_delta, params, momentum):
    islands = lax.axis_size("island")
    inner = lax.axis_size("inner")
    count = 2 * D * KVH * HEAD
    average, sq = all_reduce(island_delta[0], islands, inner)
    return outer_update(average, params, momentum, sq[0, 0] / count)


def solution(mesh):
    in_specs = (P("island", None, "inner", None), P(None, "inner", None), P(None, "inner", None))
    out_specs = (P(None, "inner", None), P(None, "inner", None))
    return jax.shard_map(body, mesh=mesh, in_specs=in_specs, out_specs=out_specs, check_vma=False)
```
